32 devices in a mesh: grp: 2 (over y), gx: 4 (over z), gy: 2 (over x), gz: 2 (over core).
Axes of the slice: x: 2, y: 2, z: 4, core: 2. Of those that a mesh axis runs over, the one named last changes fastest.
Arguments:
- basis_modes: float32 [128, 64, 16, 256], P(None, ('grp', 'gx'), 'gy', 'gz'), parts along dimension 1, may hold values from -13 to 13
- reduced_state: float32 [256, 32], P('grp'), parts along dimension 0, may hold values from -0.6 to 0.6
- fine_state: bfloat16 [32, 64, 16, 256], P(None, ('grp', 'gx'), 'gy', 'gz'), parts along dimension 1, may hold values from -27 to 27
- bound_state: float32 [32, 64, 16, 256], P(None, ('grp', 'gx'), 'gy', 'gz'), parts along dimension 1, may hold values from 0 to 0.5
- velocity: float32 [64, 16, 256], P(('grp', 'gx'), 'gy', 'gz'), parts along dimension 0, may hold values from 0.1 to 0.5
- zone_labels: int32 [64, 16, 256], P(('grp', 'gx'), 'gy', 'gz'), parts along dimension 0, may hold values from 0 to 3
- capacity: float32 [3], replicated, may hold values from 0.5 to 2
- on_rate: float32 [32], replicated, may hold values from 0.02 to 0.1
- off_rate: float32 [32], replicated, may hold values from 0.02 to 0.3
- inlet_level: float32 [64], P('grp'), parts along dimension 0, may hold values from 0.5 to 5
Outputs:
- new_modes: float32 [32, 64, 16, 256], P(None, ('grp', 'gx'), 'gy', 'gz'), parts along dimension 1
- factor: float32 [64, 32], P('grp'), parts along dimension 0
- coefficients: float32 [256, 32], P('grp'), parts along dimension 0
- bound_next: float32 [32, 64, 16, 256], P(None, ('grp', 'gx'), 'gy', 'gz'), parts along dimension 1
The draws below stay inside these ranges and needn't reach their ends.
There are 2 independent parts, one for each index of `grp`. The reference program is written for one: setup_inputs(seed, part) draws one part's arguments, and reference() takes and returns one part's arrays. A program takes and returns all parts, laid end to end along the dimension named above; an argument that names none is the same for every part. Nothing has to cross between parts.
All inputs are finite; a program needn't handle non-finite values.
Results may differ from the reference program's by a relative error of at most 0.0003.
Values sent between devices are 32-bit elements; how exact they have to be, the bound alone decides.
No kernel may reach another device: no remote copies, remote signals or barrier semaphores. Data moves between devices by JAX's collectives and lax.ppermute only.
A program may use at most 64 MiB of HBM per device.

```python
import math
import jax
import jax.numpy as jnp
from jax import lax

K = 128
S = 32
ZONES = 3
NX = 32
NY = 16
NZ = 256
ROWS = 131072


def draw_basis_modes(key, part):
    scale_key, sign_key, mix_key, noise_key = jax.random.split(key, 4)
    mode_scale = jnp.exp(jax.random.uniform(scale_key, (K, 1, 1, 1), jnp.float32, -0.7, 0.7))
    coupling_sign = jnp.where(jax.random.bernoulli(sign_key, 0.5, (K, 1, 1, 1)), 1.0, -1.0)
    coupling = jax.random.uniform(mix_key, (K, 1, 1, 1), jnp.float32, 0.3, 0.6) * coupling_sign
    noise = jax.random.truncated_normal(noise_key, -4.0, 4.0, (K + 1, NX, NY, NZ), jnp.float32)
    return (mode_scale * (noise[:K] + coupling * noise[1:])).astype(jnp.float32)


def draw_fine_state(key, part):
    amplitude_key, rough_key = jax.random.split(key, 2)
    amplitude = jnp.exp(jax.random.uniform(amplitude_key, (S, 1, 1, 1), jnp.float32, math.log(0.3), math.log(3.0)))
    position = jnp.arange(NX, dtype=jnp.float32) / max(NX - 1, 1)
    region = (0.3 * jnp.power(10.0, position))[None, :, None, None]
    roughness = jax.random.truncated_normal(rough_key, -3.0, 3.0, (S, NX, NY, NZ), jnp.float32)
    return (amplitude * region * roughness).astype(jnp.bfloat16)


def with_ends(result, own_key, smallest, largest):
    index_at = [jax.random.randint(jax.random.fold_in(own_key, axis), (), 0, length) for axis, length in enumerate(result.shape)]
    widest = result.shape.index(max(result.shape))
    next_to = index_at[:widest] + [(index_at[widest] + 1) % result.shape[widest]] + index_at[widest + 1:]
    return result.at[tuple(index_at)].set(smallest).at[tuple(next_to)].set(largest)


def levels(own_key, shape, pieces, smallest, high):
    gain = 1.0
    for dim, blocks in pieces:
        steps = jax.random.uniform(jax.random.fold_in(jax.random.fold_in(own_key, 6), dim), (blocks,), jnp.float32, smallest / len(pieces), high / len(pieces))
        gain = gain * jnp.repeat(jnp.exp(steps), shape[dim] // blocks).reshape((-1,) + (1,) * (len(shape) - 1 - dim))
    return gain


def normal_values(own_key, shape, scale, most, kind=jnp.bfloat16):
    return jnp.clip(scale * jax.random.normal(own_key, shape, jnp.float32), -most, most).astype(kind)


def setup_inputs(seed: int = 0, part: int = 0) -> dict:
    seeds = jax.random.split(jax.random.key(seed), 11)
    part_splits = jax.random.split(jax.random.fold_in(seeds[10], part), 11)
    return {
        "basis_modes": draw_basis_modes(jax.random.fold_in(jax.random.fold_in(seeds[10], part), 71), part),
        "reduced_state": normal_values(part_splits[1], (K, S), 0.1, 0.6, jnp.float32),
        "fine_state": draw_fine_state(jax.random.fold_in(jax.random.fold_in(seeds[10], part), 71), part),
        "bound_state": jnp.clip(0.5 * jax.random.uniform(part_splits[3], (S, NX, NY, NZ), jnp.float32) ** levels(part_splits[3], (S, NX, NY, NZ), ((1, 4), (2, 2), (3, 2)), -0.2, 0.2), 0.0, 0.5),
        "velocity": jnp.clip(0.1 + 0.4 * jax.random.uniform(part_splits[4], (NX, NY, NZ), jnp.float32) ** levels(part_splits[4], (NX, NY, NZ), ((0, 4), (1, 2), (2, 2)), -0.2, 0.2), 0.1, 0.5),
        "zone_labels": with_ends(jax.random.randint(part_splits[5], (NX, NY, NZ), 0, 4), jax.random.fold_in(part_splits[5], 1), 0, 3).astype(jnp.int32),
        "capacity": jnp.clip(jnp.exp(jax.random.uniform(seeds[6], (ZONES,), jnp.float32, math.log(0.5), math.log(2.0))), 0.5, 2.0),
        "on_rate": jnp.clip(jnp.exp(jax.random.uniform(seeds[7], (S,), jnp.float32, math.log(0.02), math.log(0.1))), 0.02, 0.1),
        "off_rate": jnp.clip(jnp.exp(jax.random.uniform(seeds[8], (S,), jnp.float32, math.log(0.02), math.log(0.3))), 0.02, 0.3),
        "inlet_level": jnp.clip(jnp.exp(jax.random.uniform(part_splits[9], (S,), jnp.float32, math.log(0.5), math.log(5.0))), 0.5, 5.0),
    }


highest = lax.Precision.HIGHEST
diffusion_number = 0.03

def capacity_map(zone_labels, capacity):
    cap_field = jnp.zeros(zone_labels.shape, jnp.float32)
    for zone_index in range(capacity.shape[0]):
        cap_field = cap_field + jnp.where(zone_labels == zone_index + 1, capacity[zone_index], 0.0)
    return cap_field

def pad_field(analyte, inlet_level):
    padded = jnp.pad(analyte, ((0, 0), (1, 1), (1, 1), (1, 1)), mode='edge')
    inlet_plane = jnp.broadcast_to(inlet_level[:, None, None, None], (padded.shape[0], 1, padded.shape[2], padded.shape[3]))
    return jnp.concatenate([inlet_plane.astype(padded.dtype), padded[:, 1:]], axis=1)

def advance(padded, bound_now, velocity, cap_field, on_rate, off_rate):
    centre = padded[:, 1:-1, 1:-1, 1:-1]
    behind = padded[:, :-2, 1:-1, 1:-1]
    beside = behind + padded[:, 2:, 1:-1, 1:-1] + padded[:, 1:-1, :-2, 1:-1] + padded[:, 1:-1, 2:, 1:-1]
    beside = beside + padded[:, 1:-1, 1:-1, :-2] + padded[:, 1:-1, 1:-1, 2:]
    surface = jnp.where(cap_field > 0.0, 1.0, 0.0)
    reaction = surface * (on_rate[:, None, None, None] * centre * (cap_field - bound_now) - off_rate[:, None, None, None] * bound_now)
    moved = centre + diffusion_number * (beside - 6.0 * centre) - velocity * (centre - behind) - reaction
    return (moved, bound_now + reaction)

def contract_cells(left_rows, right_rows):
    return lax.dot_general(left_rows.astype(jnp.float32), right_rows.astype(jnp.float32), (((1,), (1,)), ((), ())), precision=highest, preferred_element_type=jnp.float32)

def reference(basis_modes, reduced_state, fine_state, bound_state, velocity, zone_labels, capacity, on_rate, off_rate, inlet_level):
    cap_field = capacity_map(zone_labels, capacity)
    analyte = jnp.einsum('ks,kxyz->sxyz', reduced_state, basis_modes, precision=highest) + fine_state.astype(jnp.float32)
    bound_now = bound_state
    for step_index in range(2):
        analyte, bound_now = advance(pad_field(analyte, inlet_level), bound_now, velocity, cap_field, on_rate, off_rate)
    inverse_rows = 1.0 / ROWS
    snapshot_rows = analyte.reshape(S, ROWS)
    basis_rows = basis_modes.reshape(K, ROWS)
    coefficients = contract_cells(basis_rows, snapshot_rows) * inverse_rows
    residual = snapshot_rows - lax.dot_general(coefficients.astype(jnp.float32), basis_rows.astype(jnp.float32), (((0,), (0,)), ((), ())), precision=highest, preferred_element_type=jnp.float32)
    gram_sum = contract_cells(residual, residual) * inverse_rows
    lower_factor = jnp.linalg.cholesky(gram_sum)
    new_modes = jax.scipy.linalg.solve_triangular(lower_factor, residual, lower=True)
    return (new_modes.reshape(S, NX, NY, NZ), lower_factor.T, coefficients, bound_now)
```

```python
import functools

import jax
import jax.numpy as jnp
from jax import lax
from jax.experimental import pallas as pl
from jax.experimental.pallas import tpu as pltpu
from jax.sharding import PartitionSpec as P

highest = lax.Precision.HIGHEST
diffusion_number = 0.03
f32 = jnp.float32
bf16 = jnp.bfloat16


def split(value):
    high = value.astype(bf16)
    return high, (value - high.astype(f32)).astype(bf16)


def mm(a, b):
    return jnp.dot(a, b, preferred_element_type=f32)


def mm_nt(a, b):
    return lax.dot_general(a, b, (((1,), (1,)), ((), ())), preferred_element_type=f32)


def mm_exact(a, b):
    return jnp.dot(a, b, precision=highest, preferred_element_type=f32)


def face_count(axis):
    size = lax.axis_size(axis)
    return 0 if size == 1 else 1 if size == 2 else 2


def store_pair(refs, axis, low, high, put):
    if len(refs) == 1:
        put(refs[0], jnp.where(lax.axis_index(axis) == 0, high, low))
    elif len(refs) == 2:
        put(refs[0], low)
        put(refs[1], high)


def put_lanes(start, size):
    def put(ref, value):
        ref[:, pl.ds(start, size)] = value

    return put


def pack_column(refs, axis, tile, cell):
    lanes = tile.shape[1]
    here = lax.broadcasted_iota(jnp.int32, tile.shape, 1) == cell

    def put(ref, shift):
        ref[...] = jnp.where(here, pltpu.roll(tile, shift, 1), ref[...])

    if len(refs) == 1:
        high = lax.axis_index(axis) == 0
        put(refs[0], jnp.where(high, lax.rem(cell + 1, lanes), cell))
    elif len(refs) == 2:
        put(refs[0], cell)
        put(refs[1], lax.rem(cell + 1, lanes))


def emit_faces(faces, slab, x, shape):
    _, nx, ny, nz = shape
    xf, yf, zf = faces

    @pl.when(x == 0)
    def _():
        if len(xf) == 2:
            xf[0][...] = slab
        elif len(xf) == 1:
            xf[0][...] = slab

    @pl.when(x == nx - 1)
    def _():
        if len(xf) == 2:
            xf[1][...] = slab
        elif len(xf) == 1:

            @pl.when(lax.axis_index("gx") == 0)
            def _():
                xf[0][...] = slab

    store_pair(yf, "gy", slab[:, :nz], slab[:, -nz:], put_lanes(pl.multiple_of(x * nz, nz), nz))
    for y in range(ny):
        pack_column(zf, "gz", slab[:, y * nz : (y + 1) * nz], x * ny + y)


def face_shapes(shape):
    ns, nx, ny, nz = shape
    return (
        [(ns, ny * nz)] * face_count("gx"),
        [(ns, nx * nz)] * face_count("gy"),
        [(ns, nz)] * face_count("gz"),
    )


def unflatten(flat, shape):
    out = []
    for axis in ("gx", "gy", "gz"):
        n = face_count(axis)
        out.append(list(flat[:n]))
        flat = flat[n:]
    return out, flat


def exchange(faces):
    got = []
    for axis, sent in zip(("gx", "gy", "gz"), faces, strict=True):
        size = lax.axis_size(axis)
        if len(sent) == 1:
            got.append([lax.ppermute(sent[0], axis, [(0, 1), (1, 0)])])
        elif len(sent) == 2:
            up = [(i, i + 1) for i in range(size - 1)]
            down = [(j, i) for i, j in up]
            got.append([lax.ppermute(sent[1], axis, up), lax.ppermute(sent[0], axis, down)])
        else:
            got.append([])
    return got


def start_kernel(shape, nk, reduced, basis, fine, out_a, out_b, *rest):
    ns, nx, ny, nz = shape
    faces, (rows,) = unflatten(rest, shape)
    x = pl.program_id(0)

    @pl.when(x == 0)
    def _():
        for ref in faces[2]:
            ref[...] = jnp.zeros(ref.shape, f32)

    r_high, r_low = split(reduced[...].T)
    flat = basis.reshape(nk * ny, nz)
    rows[...] = fine[...].reshape(ns * ny, nz).astype(f32)
    tiles = []
    for y in range(ny):
        high, low = split(flat[pl.ds(y, nk, stride=ny), :])
        out_b[:nk, y * nz : (y + 1) * nz] = high
        out_b[nk:, y * nz : (y + 1) * nz] = low
    both = out_b[...]
    slab = mm(jnp.concatenate([r_high, r_high], axis=1), both) + mm(r_low, both[:nk])
    for y in range(ny):
        tiles.append(slab[:, y * nz : (y + 1) * nz] + rows[pl.ds(y, ns, stride=ny), :])
    slab = jnp.concatenate(tiles, axis=1)
    out_a[...] = slab
    emit_faces(faces, slab, x, shape)


def start(reduced, basis, fine):
    nk = basis.shape[0]
    ns, nx, ny, nz = shape = fine.shape
    whole = lambda s: pl.BlockSpec(s, lambda x: (0,) * len(s))
    groups = [s for g in face_shapes(shape) for s in g]
    outs = pl.pallas_call(
        functools.partial(start_kernel, shape, nk),
        grid=(nx,),
        in_specs=[
            whole((nk, ns)),
            pl.BlockSpec((nk, 1, ny, nz), lambda x: (0, x, 0, 0)),
            pl.BlockSpec((ns, 1, ny, nz), lambda x: (0, x, 0, 0)),
        ],
        out_specs=[
            pl.BlockSpec((ns, ny * nz), lambda x: (0, x)),
            pl.BlockSpec((2 * nk, ny * nz), lambda x: (0, x)),
        ]
        + [whole(s) for s in groups],
        out_shape=[
            jax.ShapeDtypeStruct((ns, nx * ny * nz), f32),
            jax.ShapeDtypeStruct((2 * nk, nx * ny * nz), bf16),
        ]
        + [jax.ShapeDtypeStruct(s, f32) for s in groups],
        scratch_shapes=[pltpu.VMEM((ns * ny, nz), f32)],
        name="start",
    )(reduced, basis, fine)
    faces, _ = unflatten(outs[2:], shape)
    return outs[0], outs[1], faces


def bb_kernel(nk, both, out):
    i = pl.program_id(0)
    product = mm_nt(both[:nk, :], both[...])
    mixed = product[:, nk:]
    product = product[:, :nk] + mixed + mixed.T

    @pl.when(i == 0)
    def _():
        out[...] = product

    @pl.when(i > 0)
    def _():
        out[...] = out[...] + product


def basis_products(both, steps):
    nk = both.shape[0] // 2
    return pl.pallas_call(
        functools.partial(bb_kernel, nk),
        grid=(steps,),
        in_specs=[pl.BlockSpec((2 * nk, both.shape[1] // steps), lambda i: (0, i))],
        out_specs=pl.BlockSpec((nk, nk), lambda i: (0, 0)),
        out_shape=jax.ShapeDtypeStruct((nk, nk), f32),
        name="basis_products",
    )(both)


def beside_of(got, at_start):
    return got[0] if len(got) == 1 else got[0 if at_start else 1]


def stencil(shape, x, pad, y_got, z_got, bound_tile, store, args):
    velocity, zone_labels, capacity, rates = args
    ns, nx, ny, nz = shape
    first = {a: lax.axis_index(a) == 0 for a in ("gy", "gz")}
    last = {a: lax.axis_index(a) == lax.axis_size(a) - 1 for a in ("gy", "gz")}
    labels = zone_labels[x]
    cap_slab = jnp.zeros(labels.shape, f32)
    for zone in range(capacity.shape[0]):
        cap_slab = cap_slab + jnp.where(labels == zone + 1, capacity[zone], 0.0)
    surface_slab = jnp.where(cap_slab > 0.0, 1.0, 0.0)
    velocity_slab = velocity[x]
    on = jnp.broadcast_to(rates[:, 0:1], (ns, nz))
    off = jnp.broadcast_to(rates[:, 1:2], (ns, nz))
    lane = lax.broadcasted_iota(jnp.int32, (ns, nz), 1)
    x_at = pl.multiple_of(x * nz, nz)
    left, right = lane == 0, lane == nz - 1
    slabs = []
    for y in range(ny):
        at = pl.multiple_of(x * ny * nz, nz) + y * nz
        tile = lambda slabs_on, rows_on: pad[
            :, pl.ds(pl.multiple_of(at + (slabs_on * ny + rows_on) * nz, nz), nz)
        ]
        centre, behind, ahead = tile(1, 0), tile(0, 0), tile(2, 0)
        if y > 0:
            y_low = tile(1, -1)
        elif y_got:
            y_low = jnp.where(first["gy"], centre, beside_of(y_got, True)[:, pl.ds(x_at, nz)])
        else:
            y_low = centre
        if y < ny - 1:
            y_high = tile(1, 1)
        elif y_got:
            y_high = jnp.where(last["gy"], centre, beside_of(y_got, False)[:, pl.ds(x_at, nz)])
        else:
            y_high = centre
        z_low, z_high = pltpu.roll(centre, 1, 1), pltpu.roll(centre, nz - 1, 1)
        cell = x * ny + y
        edge_low = edge_high = centre
        if len(z_got) == 1:
            shift = jnp.where(first["gz"], nz - 1 - cell, lax.rem(nz - cell, nz))
            beside = pltpu.roll(z_got[0][...], shift, 1)
            edge_low = jnp.where(first["gz"], centre, beside)
            edge_high = jnp.where(first["gz"], beside, centre)
        elif len(z_got) == 2:
            beside = pltpu.roll(z_got[0][...], lax.rem(nz - cell, nz), 1)
            edge_low = jnp.where(first["gz"], centre, beside)
            beside = pltpu.roll(z_got[1][...], nz - 1 - cell, 1)
            edge_high = jnp.where(last["gz"], centre, beside)
        z_low = jnp.where(left, edge_low, z_low)
        z_high = jnp.where(right, edge_high, z_high)
        near = behind + ahead + y_low + y_high + z_low + z_high
        row = lambda slab: jnp.broadcast_to(slab[y : y + 1], (ns, nz))
        bound_now = bound_tile(cell, y)
        reaction = row(surface_slab) * (
            on * centre * (row(cap_slab) - bound_now) - off * bound_now
        )
        moved = (
            centre
            + diffusion_number * (near - 6.0 * centre)
            - row(velocity_slab) * (centre - behind)
            - reaction
        )
        store(cell, y, bound_now + reaction)
        slabs.append(moved)
    return jnp.concatenate(slabs, axis=1)


def fill_pad(shape, pad, analyte, x_got, rates):
    ns, nx, ny, nz = shape
    slab = ny * nz
    pad[:, slab : (nx + 1) * slab] = analyte[...]
    at_inlet = lax.axis_index("gx") == 0
    at_outlet = lax.axis_index("gx") == lax.axis_size("gx") - 1
    inlet = jnp.broadcast_to(rates[:, 2:3], (ns, slab))
    outlet = analyte[:, (nx - 1) * slab :]
    if x_got:
        pad[:, :slab] = jnp.where(at_inlet, inlet, beside_of(x_got, True)[...])
        pad[:, (nx + 1) * slab :] = jnp.where(at_outlet, outlet, beside_of(x_got, False)[...])
    else:
        pad[:, :slab] = inlet
        pad[:, (nx + 1) * slab :] = outlet


def first_kernel(shape, analyte, bound, velocity, zone_labels, capacity, rates, *rest):
    ns, nx, ny, nz = shape
    got, rest = unflatten(rest, shape)
    out_a, out_bound = rest[:2]
    faces, (pad,) = unflatten(rest[2:], shape)
    fill_pad(shape, pad, analyte, got[0], rates)
    for ref in faces[2]:
        ref[...] = jnp.zeros(ref.shape, f32)

    def body(x, carry):
        def bound_tile(cell, y):
            return bound[pl.ds(cell, ns, stride=nx * ny), :]

        def store(cell, y, value):
            out_bound[:, pl.ds(pl.multiple_of(cell * nz, nz), nz)] = value

        slab = stencil(
            shape, x, pad, got[1], got[2], bound_tile, store, (velocity, zone_labels, capacity, rates)
        )
        out_a[:, pl.ds(pl.multiple_of(x * ny * nz, ny * nz), ny * nz)] = slab
        emit_faces(faces, slab, x, shape)
        return carry

    lax.fori_loop(0, nx, body, 0)


def second_kernel(shape, nk, analyte, bound, velocity, zone_labels, capacity, rates, both, bb, *rest):
    ns, nx, ny, nz = shape
    got, rest = unflatten(rest, shape)
    out_s, out_bound, out_totals, pad = rest
    fill_pad(shape, pad, analyte, got[0], rates)

    def body(x, carry):
        def bound_tile(cell, y):
            return bound[:, pl.ds(pl.multiple_of(cell * nz, nz), nz)]

        def store(cell, y, value):
            out_bound[pl.ds(cell, ns, stride=nx * ny), :] = value

        slab = stencil(
            shape, x, pad, got[1], got[2], bound_tile, store, (velocity, zone_labels, capacity, rates)
        )
        high, low = split(slab)
        at = pl.ds(pl.multiple_of(x * ny * nz, ny * nz), ny * nz)
        out_s[:ns, at] = high
        out_s[ns:, at] = low
        return carry

    lax.fori_loop(0, nx, body, 0)
    snap = out_s[...]
    product = mm_nt(snap, both[...])
    out_totals[:ns, :] = product[:ns, :nk] + product[:ns, nk:] + product[ns:, :nk]
    square = mm_nt(snap, snap)
    square = square[:ns, :ns] + square[:ns, ns:] + square[ns:, :ns]
    out_totals[ns : 2 * ns, :] = jnp.concatenate(
        [square, jnp.zeros((ns, nk - ns), f32)], axis=1
    )
    out_totals[2 * ns :, :] = bb[...]


def step_call(kernel, shape, operands, got, out_shape, name):
    ns, nx, ny, nz = shape
    smem = {4}
    flat = [g for group in got for g in group]
    in_specs = [
        pl.BlockSpec(memory_space=pltpu.SMEM if i in smem else pltpu.VMEM)
        for i in range(len(operands) + len(flat))
    ]
    return pl.pallas_call(
        kernel,
        in_specs=in_specs,
        out_specs=[pl.BlockSpec(memory_space=pltpu.VMEM) for _ in out_shape],
        out_shape=out_shape,
        scratch_shapes=[pltpu.VMEM((ns, (nx + 2) * ny * nz), f32)],
        name=name,
    )(*operands, *flat)


def finish_kernel(shape, nk, inverse_rows, totals, snap, both, out_modes, out_factor, out_coeffs, left_b, left_s):
    ns, nx, ny, nz = shape

    @pl.when(pl.program_id(0) == 0)
    def _():
        coeffs = totals[:ns, :] * inverse_rows
        out_coeffs[...] = coeffs.T
        weighted = mm_exact(coeffs, totals[2 * ns :, :] * inverse_rows)
        mixed = lax.dot_general(
            coeffs, coeffs, (((1,), (1,)), ((), ())), precision=highest, preferred_element_type=f32
        )
        double = lax.dot_general(
            weighted, coeffs, (((1,), (1,)), ((), ())), precision=highest, preferred_element_type=f32
        )
        gram = totals[ns : 2 * ns, :ns] * inverse_rows - mixed - mixed + double
        sub = lax.broadcasted_iota(jnp.int32, (ns, 2 * ns), 0)
        lane = lax.broadcasted_iota(jnp.int32, (ns, 2 * ns), 1)
        unit = jnp.where(sub[:, :ns] == lane[:, :ns], 1.0, 0.0)
        work = jnp.concatenate([gram, unit], axis=1)
        for j in range(ns):
            row = work[j : j + 1, :]
            scale = work[:, j : j + 1] / row[:, j : j + 1]
            work = work - jnp.where(sub > j, scale * row, 0.0)
        pivots = jnp.sum(jnp.where(lane == sub, work, 0.0), axis=1, keepdims=True)
        work = work / jnp.sqrt(pivots)
        out_factor[...] = jnp.where(lane[:, :ns] >= sub[:, :ns], work[:, :ns], 0.0)
        inverse = work[:, ns:]
        s_high, s_low = split(inverse)
        b_high, b_low = split(-mm_exact(inverse, coeffs))
        left_b[:, :nk] = b_high
        left_b[:, nk : 2 * nk] = b_high
        left_b[:, 2 * nk :] = b_low
        left_s[:, :] = jnp.concatenate([s_high, s_high, s_low], axis=1)

    modes = mm(left_b[:, : 2 * nk], both[...]) + mm(left_b[:, 2 * nk :], both[:nk, :])
    modes = modes + mm(left_s[:, : 2 * ns], snap[...]) + mm(left_s[:, 2 * ns :], snap[:ns, :])
    flat = out_modes.reshape(ns * ny, nz)
    for y in range(ny):
        flat[pl.ds(y, ns, stride=ny), :] = modes[:, y * nz : (y + 1) * nz]


def finish(shape, inverse_rows, totals, snap, both):
    ns, nx, ny, nz = shape
    nk = both.shape[0] // 2
    whole = lambda s: pl.BlockSpec(s, lambda x: (0,) * len(s))
    return pl.pallas_call(
        functools.partial(finish_kernel, shape, nk, inverse_rows),
        grid=(nx,),
        in_specs=[
            whole(totals.shape),
            pl.BlockSpec((2 * ns, ny * nz), lambda x: (0, x)),
            pl.BlockSpec((2 * nk, ny * nz), lambda x: (0, x)),
        ],
        out_specs=[
            pl.BlockSpec((ns, 1, ny, nz), lambda x: (0, x, 0, 0)),
            whole((ns, ns)),
            whole((nk, ns)),
        ],
        out_shape=[
            jax.ShapeDtypeStruct(shape, f32),
            jax.ShapeDtypeStruct((ns, ns), f32),
            jax.ShapeDtypeStruct((nk, ns), f32),
        ],
        scratch_shapes=[pltpu.VMEM((ns, 3 * nk), bf16), pltpu.VMEM((ns, 3 * ns), bf16)],
        name="finish",
    )(totals, snap, both)


def sum_over(value, axes):
    for axis in axes:
        size = lax.axis_size(axis)
        if size & (size - 1):
            value = lax.psum(value, axis)
            continue
        stride = 1
        while stride < size:
            value = value + lax.ppermute(value, axis, [(i, i ^ stride) for i in range(size)])
            stride *= 2
    return value


def on_device(
    basis_modes,
    reduced_state,
    fine_state,
    bound_state,
    velocity,
    zone_labels,
    capacity,
    on_rate,
    off_rate,
    inlet_level,
):
    ns, nx, ny, nz = shape = fine_state.shape
    nk = basis_modes.shape[0]
    cells = nx * ny * nz
    rates = jnp.stack([on_rate, off_rate, inlet_level], axis=1)
    analyte, both, faces = start(reduced_state, basis_modes, fine_state)
    got = exchange(faces)
    bb = basis_products(both, 4)
    fields = [velocity, zone_labels, capacity, rates]
    struct = jax.ShapeDtypeStruct
    outs = step_call(
        functools.partial(first_kernel, shape),
        shape,
        [analyte, bound_state.reshape(ns * nx * ny, nz)] + fields,
        got,
        [struct((ns, cells), f32), struct((ns, cells), f32)]
        + [struct(s, f32) for g in face_shapes(shape) for s in g],
        "first_step",
    )
    faces, _ = unflatten(outs[2:], shape)
    got = exchange(faces)
    snap, bound_next, totals = step_call(
        functools.partial(second_kernel, shape, nk),
        shape,
        [outs[0], outs[1]] + fields + [both, bb],
        got,
        [
            struct((2 * ns, cells), bf16),
            struct((ns * nx * ny, nz), f32),
            struct((2 * ns + nk, nk), f32),
        ],
        "second_step",
    )
    totals = sum_over(totals, ("gz", "gy", "gx"))
    inverse_rows = 1.0 / (
        cells * lax.axis_size("gx") * lax.axis_size("gy") * lax.axis_size("gz")
    )
    modes, factor, coeffs = finish(shape, inverse_rows, totals, snap, both)
    return (modes, factor, coeffs, bound_next.reshape(shape))


def solution(mesh):
    return jax.shard_map(
        on_device,
        mesh=mesh,
        in_specs=(
            P(None, ("grp", "gx"), "gy", "gz"),
            P("grp", None),
            P(None, ("grp", "gx"), "gy", "gz"),
            P(None, ("grp", "gx"), "gy", "gz"),
            P(("grp", "gx"), "gy", "gz"),
            P(("grp", "gx"), "gy", "gz"),
            P(),
            P(),
            P(),
            P("grp"),
        ),
        out_specs=(
            P(None, ("grp", "gx"), "gy", "gz"),
            P("grp", None),
            P("grp", None),
            P(None, ("grp", "gx"), "gy", "gz"),
        ),
        check_vma=False,
    )
```

```python
import functools

import jax
import jax.numpy as jnp
from jax import lax
from jax.experimental import pallas as pl
from jax.experimental.pallas import tpu as pltpu
from jax.sharding import PartitionSpec as P

highest = lax.Precision.HIGHEST
diffusion_number = 0.03
f32 = jnp.float32
bf16 = jnp.bfloat16
vmem_limit = 16 << 20


def split(value):
    high = value.astype(bf16)
    return high, (value - high.astype(f32)).astype(bf16)


def mm(a, b):
    return jnp.dot(a, b, preferred_element_type=f32)


def mm_nt(a, b):
    return lax.dot_general(a, b, (((1,), (1,)), ((), ())), preferred_element_type=f32)


def mm_exact(a, b):
    return jnp.dot(a, b, precision=highest, preferred_element_type=f32)


def face_count(axis):
    size = lax.axis_size(axis)
    return 0 if size == 1 else 1 if size == 2 else 2


def pack_column(packed, axis, tile, cell):
    lanes = tile.shape[1]
    here = lax.broadcasted_iota(jnp.int32, tile.shape, 1) == cell
    after = lax.rem(cell + 1, lanes)
    if len(packed) == 1:
        shifts = [jnp.where(lax.axis_index(axis) == 0, after, cell)]
    else:
        shifts = [cell, after]
    return [jnp.where(here, pltpu.roll(tile, s, 1), p) for p, s in zip(packed, shifts)]


def copy_faces(faces, field, shape):
    _, nx, ny, nz = shape
    slab = ny * nz
    for refs, axis, width, count, last in (
        (faces[0], "gx", slab, 1, (nx - 1) * slab),
        (faces[1], "gy", nz, nx, slab - nz),
    ):
        for i, ref in enumerate(refs):
            if len(refs) == 1:
                at = pl.multiple_of(jnp.where(lax.axis_index(axis) == 0, last, 0), nz)
            else:
                at = last * i
            for j in range(count):
                ref[:, j * width : (j + 1) * width] = field[:, pl.ds(at + j * slab, width)]


def face_shapes(shape):
    ns, nx, ny, nz = shape
    return (
        [(ns, ny * nz)] * face_count("gx"),
        [(ns, nx * nz)] * face_count("gy"),
        [(ns, nz)] * face_count("gz"),
    )


def unflatten(flat, shape):
    out = []
    for axis in ("gx", "gy", "gz"):
        n = face_count(axis)
        out.append(list(flat[:n]))
        flat = flat[n:]
    return out, flat


def exchange(faces):
    got = []
    for axis, sent in zip(("gx", "gy", "gz"), faces, strict=True):
        size = lax.axis_size(axis)
        if len(sent) == 1:
            got.append([lax.ppermute(sent[0], axis, [(0, 1), (1, 0)])])
        elif len(sent) == 2:
            up = [(i, i + 1) for i in range(size - 1)]
            down = [(j, i) for i, j in up]
            got.append([lax.ppermute(sent[1], axis, up), lax.ppermute(sent[0], axis, down)])
        else:
            got.append([])
    return got


def start_kernel(shape, nk, reduced, basis, fine, out_a, out_b, out_bb, *rest):
    ns, nx, ny, nz = shape
    faces, scratch = unflatten(rest, shape)
    r_buf, b_buf, f_buf, rows, both, r_sem, b_sem, f_sem, o_sem = scratch
    slab_at = lambda x: pl.ds(pl.multiple_of(x * ny * nz, ny * nz), ny * nz)
    o_copy = lambda x: pltpu.make_async_copy(both.at[:, slab_at(x)], out_b.at[:, slab_at(x)], o_sem.at[x])
    r_copy = pltpu.make_async_copy(reduced, r_buf, r_sem)
    f_copy = pltpu.make_async_copy(fine, f_buf, f_sem)
    b_copy = lambda x: pltpu.make_async_copy(basis.at[:, x], b_buf.at[x], b_sem.at[x])
    r_copy.start()
    b_copy(0).start()
    f_copy.start()
    for x in range(1, nx):
        b_copy(x).start()
    r_copy.wait()
    r_high, r_low = split(r_buf[...])
    r_twice = jnp.concatenate([r_high, r_high], axis=1)
    group = max(1, min(ny, 256 // nz))

    def body(x, packed):
        b_copy(x).wait()

        @pl.when(x == 0)
        def _():
            f_copy.wait()

        flat = b_buf.at[x].reshape(nk * ny, nz)
        rows[...] = f_buf[:, pl.ds(x, 1)].reshape(ns * ny, nz).astype(f32)
        for y in range(0, ny, group):
            at = pl.multiple_of(x * ny * nz, ny * nz) + y * nz
            parts = [split(flat[pl.ds(y + i, nk, stride=ny), :]) for i in range(group)]
            high = jnp.concatenate([p[0] for p in parts], axis=1)
            low = jnp.concatenate([p[1] for p in parts], axis=1)
            both[:nk, pl.ds(at, group * nz)] = high
            both[nk:, pl.ds(at, group * nz)] = low
            slab = mm(r_twice, jnp.concatenate([high, low], axis=0)) + mm(r_low, high)
            for i in range(group):
                tile = slab[:, i * nz : (i + 1) * nz] + rows[pl.ds(y + i, ns, stride=ny), :]
                out_a[:, pl.ds(at + i * nz, nz)] = tile
                packed = pack_column(packed, "gz", tile, x * ny + y + i)
        o_copy(x).start()
        return packed

    packed = lax.fori_loop(0, nx, body, [jnp.zeros((ns, nz), f32) for _ in faces[2]])
    for ref, value in zip(faces[2], packed):
        ref[...] = value
    copy_faces(faces, out_a, shape)
    product = mm_nt(both[:nk, :], both[...])
    mixed = product[:, nk:]
    out_bb[...] = product[:, :nk] + mixed + mixed.T
    for x in range(nx):
        o_copy(x).wait()


def start(reduced, basis, fine):
    nk = basis.shape[0]
    ns, nx, ny, nz = shape = fine.shape
    groups = [s for g in face_shapes(shape) for s in g]
    outs = pl.pallas_call(
        functools.partial(start_kernel, shape, nk),
        in_specs=[pl.BlockSpec(memory_space=pltpu.HBM)] * 3,
        out_specs=[
            pl.BlockSpec(memory_space=pltpu.HBM if i == 1 else pltpu.VMEM)
            for i in range(3 + len(groups))
        ],
        out_shape=[
            jax.ShapeDtypeStruct((ns, nx * ny * nz), f32),
            pltpu.HBM((2 * nk, nx * ny * nz), bf16),
            jax.ShapeDtypeStruct((nk, nk), f32),
        ]
        + [jax.ShapeDtypeStruct(s, f32) for s in groups],
        scratch_shapes=[
            pltpu.VMEM((ns, nk), f32),
            pltpu.VMEM((nx, nk, ny, nz), f32),
            pltpu.VMEM((ns, nx, ny, nz), bf16),
            pltpu.VMEM((ns * ny, nz), f32),
            pltpu.VMEM((2 * nk, nx * ny * nz), bf16),
            pltpu.SemaphoreType.DMA,
            pltpu.SemaphoreType.DMA((nx,)),
            pltpu.SemaphoreType.DMA,
            pltpu.SemaphoreType.DMA((nx,)),
        ],
        compiler_params=pltpu.CompilerParams(vmem_limit_bytes=vmem_limit),
        name="start",
    )(*[pltpu.with_memory_space_constraint(a, pltpu.HBM) for a in (reduced, basis, fine)])
    faces, _ = unflatten(outs[3:], shape)
    return outs[:3], faces


def beside_of(got, at_start):
    return got[0] if len(got) == 1 else got[0 if at_start else 1]


def stencil(shape, x, pad, y_got, z_got, bound_tile, store, args):
    velocity, zone_labels, capacity, rates = args
    ns, nx, ny, nz = shape
    first = {a: lax.axis_index(a) == 0 for a in ("gy", "gz")}
    last = {a: lax.axis_index(a) == lax.axis_size(a) - 1 for a in ("gy", "gz")}
    labels = zone_labels[x]
    cap_slab = jnp.zeros(labels.shape, f32)
    for zone in range(capacity.shape[0]):
        cap_slab = cap_slab + jnp.where(labels == zone + 1, capacity[zone], 0.0)
    surface_slab = jnp.where(cap_slab > 0.0, 1.0, 0.0)
    velocity_slab = velocity[x]
    on = jnp.broadcast_to(rates[:, 0:1], (ns, nz))
    off = jnp.broadcast_to(rates[:, 1:2], (ns, nz))
    lane = lax.broadcasted_iota(jnp.int32, (ns, nz), 1)
    x_at = pl.multiple_of(x * nz, nz)
    left, right = lane == 0, lane == nz - 1
    inner = lane == jnp.where(first["gz"], nz - 1, 0)
    inner_low = lane == jnp.where(first["gz"], -1, 0)
    inner_high = lane == jnp.where(last["gz"], -1, nz - 1)
    for y in range(ny):
        at = pl.multiple_of(x * ny * nz, nz) + y * nz
        tile = lambda slabs_on, rows_on: pad[
            :, pl.ds(pl.multiple_of(at + (slabs_on * ny + rows_on) * nz, nz), nz)
        ]
        centre, behind, ahead = tile(1, 0), tile(0, 0), tile(2, 0)
        if y > 0:
            y_low = tile(1, -1)
        elif y_got:
            y_low = jnp.where(first["gy"], centre, beside_of(y_got, True)[:, pl.ds(x_at, nz)])
        else:
            y_low = centre
        if y < ny - 1:
            y_high = tile(1, 1)
        elif y_got:
            y_high = jnp.where(last["gy"], centre, beside_of(y_got, False)[:, pl.ds(x_at, nz)])
        else:
            y_high = centre
        z_low, z_high = pltpu.roll(centre, 1, 1), pltpu.roll(centre, nz - 1, 1)
        cell = x * ny + y
        edge = centre
        if len(z_got) == 1:
            shift = jnp.where(first["gz"], nz - 1 - cell, lax.rem(nz - cell, nz))
            edge = jnp.where(inner, pltpu.roll(z_got[0][...], shift, 1), edge)
        elif len(z_got) == 2:
            beside = pltpu.roll(z_got[0][...], lax.rem(nz - cell, nz), 1)
            edge = jnp.where(inner_low, beside, edge)
            beside = pltpu.roll(z_got[1][...], nz - 1 - cell, 1)
            edge = jnp.where(inner_high, beside, edge)
        z_low = jnp.where(left, edge, z_low)
        z_high = jnp.where(right, edge, z_high)
        near = behind + ahead + y_low + y_high + z_low + z_high
        row = lambda slab: jnp.broadcast_to(slab[y : y + 1], (ns, nz))
        bound_now = bound_tile(cell, at)
        reaction = row(surface_slab) * (
            on * centre * (row(cap_slab) - bound_now) - off * bound_now
        )
        moved = (
            centre
            + diffusion_number * (near - 6.0 * centre)
            - row(velocity_slab) * (centre - behind)
            - reaction
        )
        store(cell, at, moved, bound_now + reaction)


def fill_pad(shape, pad, analyte, x_got, rates):
    ns, nx, ny, nz = shape
    slab = ny * nz
    pad[:, slab : (nx + 1) * slab] = analyte[...]
    at_inlet = lax.axis_index("gx") == 0
    at_outlet = lax.axis_index("gx") == lax.axis_size("gx") - 1
    inlet = jnp.broadcast_to(rates[:, 2:3], (ns, slab))
    outlet = analyte[:, (nx - 1) * slab :]
    if x_got:
        pad[:, :slab] = jnp.where(at_inlet, inlet, beside_of(x_got, True)[...])
        pad[:, (nx + 1) * slab :] = jnp.where(at_outlet, outlet, beside_of(x_got, False)[...])
    else:
        pad[:, :slab] = inlet
        pad[:, (nx + 1) * slab :] = outlet


def first_kernel(shape, analyte, bound, velocity, zone_labels, capacity, rates, *rest):
    ns, nx, ny, nz = shape
    got, rest = unflatten(rest, shape)
    out_a, out_bound = rest[:2]
    faces, (pad,) = unflatten(rest[2:], shape)
    fill_pad(shape, pad, analyte, got[0], rates)

    def body(x, packed):
        packs = [packed]

        def bound_tile(cell, at):
            return bound[pl.ds(cell, ns, stride=nx * ny), :]

        def store(cell, at, moved, bound_then):
            out_bound[:, pl.ds(at, nz)] = bound_then
            out_a[:, pl.ds(at, nz)] = moved
            packs[0] = pack_column(packs[0], "gz", moved, cell)

        stencil(
            shape, x, pad, got[1], got[2], bound_tile, store, (velocity, zone_labels, capacity, rates)
        )
        return packs[0]

    packed = lax.fori_loop(0, nx, body, [jnp.zeros((ns, nz), f32) for _ in faces[2]])
    for ref, value in zip(faces[2], packed):
        ref[...] = value
    copy_faces(faces, out_a, shape)


def second_kernel(shape, nk, analyte, bound, velocity, zone_labels, capacity, rates, both, bb, *rest):
    ns, nx, ny, nz = shape
    got, rest = unflatten(rest, shape)
    out_s, out_bound, out_totals, pad, bound_buf, both_buf, sem, both_sem = rest
    both_copy = pltpu.make_async_copy(both, both_buf, both_sem)
    both_copy.start()
    fill_pad(shape, pad, analyte, got[0], rates)

    def body(x, carry):
        def bound_tile(cell, at):
            return bound[:, pl.ds(at, nz)]

        def store(cell, at, moved, bound_then):
            bound_buf[pl.ds(cell, ns, stride=nx * ny), :] = bound_then
            high, low = split(moved)
            out_s[:ns, pl.ds(at, nz)] = high
            out_s[ns:, pl.ds(at, nz)] = low

        stencil(
            shape, x, pad, got[1], got[2], bound_tile, store, (velocity, zone_labels, capacity, rates)
        )
        return carry

    lax.fori_loop(0, nx, body, 0)
    copy = pltpu.make_async_copy(bound_buf, out_bound, sem)
    copy.start()
    snap = out_s[...]
    both_copy.wait()
    product = mm_nt(snap, both_buf[...])
    out_totals[:ns, :] = product[:ns, :nk] + product[:ns, nk:] + product[ns:, :nk]
    square = mm_nt(snap, snap)
    square = square[:ns, :ns] + square[:ns, ns:] + square[ns:, :ns]
    out_totals[ns : 2 * ns, :] = jnp.concatenate(
        [square, jnp.zeros((ns, nk - ns), f32)], axis=1
    )
    out_totals[2 * ns :, :] = bb[...]
    copy.wait()


def step_call(kernel, shape, operands, got, out_shape, name, hbm=(), scratch=()):
    ns, nx, ny, nz = shape
    space = {4: pltpu.SMEM, 6: pltpu.HBM if scratch else pltpu.VMEM}
    flat = [g for group in got for g in group]
    in_specs = [
        pl.BlockSpec(memory_space=space.get(i, pltpu.VMEM))
        for i in range(len(operands) + len(flat))
    ]
    return pl.pallas_call(
        kernel,
        in_specs=in_specs,
        out_specs=[
            pl.BlockSpec(memory_space=pltpu.HBM if i in hbm else pltpu.VMEM)
            for i in range(len(out_shape))
        ],
        out_shape=out_shape,
        scratch_shapes=[pltpu.VMEM((ns, (nx + 2) * ny * nz), f32), *scratch],
        compiler_params=pltpu.CompilerParams(vmem_limit_bytes=vmem_limit),
        name=name,
    )(*operands, *flat)


def eliminate(gram, width, between):
    n = gram.shape[0]
    sub = lax.broadcasted_iota(jnp.int32, (n, 2 * n), 0)
    lane = lax.broadcasted_iota(jnp.int32, (n, 2 * n), 1)
    unit = jnp.where(sub[:, :n] == lane[:, :n], 1.0, 0.0)
    work = jnp.concatenate([gram, unit], axis=1)
    for start_at in range(0, n, width):
        columns = [
            jnp.broadcast_to(work[:, start_at + i : start_at + i + 1], (n, 2 * n))
            for i in range(width)
        ]
        for i in range(width):
            j = start_at + i
            scale = jnp.where(sub > j, columns[i] / columns[i][j : j + 1, :], 0.0)
            for k in range(i + 1, width):
                columns[k] = columns[k] - scale * columns[k][j : j + 1, :]
            work = work - scale * work[j : j + 1, :]
            between(j)
    pivots = jnp.sum(jnp.where(lane == sub, work, 0.0), axis=1, keepdims=True)
    work = work / jnp.sqrt(pivots)
    return jnp.where(lane[:, :n] >= sub[:, :n], work[:, :n], 0.0), work[:, n:]


def finish_kernel(shape, nk, inverse_rows, totals, snap, both, out_modes, out_factor, out_coeffs, *scratch):
    ns, nx, ny, nz = shape
    slab = ny * nz
    rest, modes, both_buf, sem, both_sem = scratch
    part = lambda x: slice(x * slab, (x + 1) * slab)
    both_copy = lambda x: pltpu.make_async_copy(both.at[:, part(x)], both_buf.at[:, part(x)], both_sem.at[x])
    for x in range(nx):
        both_copy(x).start()
    coeffs = totals[:ns, :] * inverse_rows
    out_coeffs[...] = coeffs
    c_high, c_low = split(coeffs)
    c_twice = jnp.concatenate([c_high, c_high], axis=1)
    weighted = mm_exact(coeffs, totals[2 * ns :, :] * inverse_rows)
    exact_nt = functools.partial(
        lax.dot_general,
        dimension_numbers=(((1,), (1,)), ((), ())),
        precision=highest,
        preferred_element_type=f32,
    )
    mixed = exact_nt(coeffs, coeffs)
    gram = totals[ns : 2 * ns, :ns] * inverse_rows - mixed - mixed + exact_nt(weighted, coeffs)

    pieces = 2 * nx if ny % 2 == 0 and 2 * nx <= ns else nx
    width = nx * slab // pieces

    def residual(j):
        if j >= pieces:
            return
        if j % (pieces // nx) == 0:
            both_copy(j // (pieces // nx)).wait()
        at = slice(j * width, (j + 1) * width)
        value = snap[:ns, at].astype(f32) + snap[ns:, at].astype(f32)
        value = value - (mm(c_twice, both_buf[:, at]) + mm(c_low, both_buf[:nk, at]))
        high, low = split(value)
        rest[:ns, at] = high
        rest[ns:, at] = low

    factor, inverse = eliminate(gram, 8 if ns % 8 == 0 else 1, residual)
    out_factor[...] = factor
    i_high, i_low = split(inverse)
    i_twice = jnp.concatenate([i_high, i_high], axis=1)
    copy = lambda x: pltpu.make_async_copy(modes.at[:, x], out_modes.at[:, x], sem.at[x])
    flat = modes.reshape(ns * nx * ny, nz)
    for x in range(nx):
        at = slice(x * slab, (x + 1) * slab)
        value = mm(i_twice, rest[:, at]) + mm(i_low, rest[:ns, at])
        for y in range(ny):
            flat[pl.ds(x * ny + y, ns, stride=nx * ny), :] = value[:, y * nz : (y + 1) * nz]
        copy(x).start()
    for x in range(nx):
        copy(x).wait()


def finish(shape, inverse_rows, totals, snap, both):
    ns, nx, ny, nz = shape
    nk = both.shape[0] // 2
    vmem = pl.BlockSpec(memory_space=pltpu.VMEM)
    return pl.pallas_call(
        functools.partial(finish_kernel, shape, nk, inverse_rows),
        in_specs=[vmem, vmem, pl.BlockSpec(memory_space=pltpu.HBM)],
        out_specs=[pl.BlockSpec(memory_space=pltpu.HBM), vmem, vmem],
        out_shape=[
            jax.ShapeDtypeStruct(shape, f32),
            jax.ShapeDtypeStruct((ns, ns), f32),
            jax.ShapeDtypeStruct((ns, nk), f32),
        ],
        scratch_shapes=[
            pltpu.VMEM((2 * ns, nx * ny * nz), bf16),
            pltpu.VMEM(shape, f32),
            pltpu.VMEM(both.shape, bf16),
            pltpu.SemaphoreType.DMA((nx,)),
            pltpu.SemaphoreType.DMA((nx,)),
        ],
        compiler_params=pltpu.CompilerParams(vmem_limit_bytes=vmem_limit),
        name="finish",
    )(totals, snap, both)


def sum_over(value, axes):
    for axis in axes:
        size = lax.axis_size(axis)
        if size & (size - 1):
            value = lax.psum(value, axis)
            continue
        stride = 1
        while stride < size:
            value = value + lax.ppermute(value, axis, [(i, i ^ stride) for i in range(size)])
            stride *= 2
    return value


def on_device(
    basis_modes,
    reduced_state,
    fine_state,
    bound_state,
    velocity,
    zone_labels,
    capacity,
    on_rate,
    off_rate,
    inlet_level,
):
    ns, nx, ny, nz = shape = fine_state.shape
    nk = basis_modes.shape[0]
    cells = nx * ny * nz
    rates = jnp.stack([on_rate, off_rate, inlet_level], axis=1)
    (analyte, both, bb), faces = start(reduced_state.T, basis_modes, fine_state)
    got = exchange(faces)
    both = pltpu.with_memory_space_constraint(both, pltpu.HBM)
    fields = [velocity, zone_labels, capacity, rates]
    struct = jax.ShapeDtypeStruct
    outs = step_call(
        functools.partial(first_kernel, shape),
        shape,
        [analyte, bound_state.reshape(ns * nx * ny, nz)] + fields,
        got,
        [struct((ns, cells), f32), struct((ns, cells), f32)]
        + [struct(s, f32) for g in face_shapes(shape) for s in g],
        "first_step",
    )
    faces, _ = unflatten(outs[2:], shape)
    got = exchange(faces)
    snap, bound_next, totals = step_call(
        functools.partial(second_kernel, shape, nk),
        shape,
        [outs[0], outs[1]] + fields + [both, bb],
        got,
        [
            struct((2 * ns, cells), bf16),
            struct((ns * nx * ny, nz), f32),
            struct((2 * ns + nk, nk), f32),
        ],
        "second_step",
        hbm=(1,),
        scratch=[
            pltpu.VMEM((ns * nx * ny, nz), f32),
            pltpu.VMEM((2 * nk, cells), bf16),
            pltpu.SemaphoreType.DMA,
            pltpu.SemaphoreType.DMA,
        ],
    )
    totals = sum_over(totals, ("gz", "gy", "gx"))
    inverse_rows = 1.0 / (
        cells * lax.axis_size("gx") * lax.axis_size("gy") * lax.axis_size("gz")
    )
    modes, factor, coeffs = finish(shape, inverse_rows, totals, snap, both)
    return (modes, factor, coeffs.T, bound_next.reshape(shape))


def solution(mesh):
    return jax.shard_map(
        on_device,
        mesh=mesh,
        in_specs=(
            P(None, ("grp", "gx"), "gy", "gz"),
            P("grp", None),
            P(None, ("grp", "gx"), "gy", "gz"),
            P(None, ("grp", "gx"), "gy", "gz"),
            P(("grp", "gx"), "gy", "gz"),
            P(("grp", "gx"), "gy", "gz"),
            P(),
            P(),
            P(),
            P("grp"),
        ),
        out_specs=(
            P(None, ("grp", "gx"), "gy", "gz"),
            P("grp", None),
            P("grp", None),
            P(None, ("grp", "gx"), "gy", "gz"),
        ),
        check_vma=False,
    )
```

```python
import functools

import jax
import jax.numpy as jnp
from jax import lax
from jax.experimental import pallas as pl
from jax.experimental.pallas import tpu as pltpu
from jax.sharding import PartitionSpec as P

highest = lax.Precision.HIGHEST
diffusion_number = 0.03
f32 = jnp.float32
bf16 = jnp.bfloat16
vmem_limit = 16 << 20


def split(value):
    high = value.astype(bf16)
    return high, (value - high.astype(f32)).astype(bf16)


def mm(a, b):
    return jnp.dot(a, b, preferred_element_type=f32)


def mm_nt(a, b):
    return lax.dot_general(a, b, (((1,), (1,)), ((), ())), preferred_element_type=f32)


def mm_exact(a, b):
    return jnp.dot(a, b, precision=highest, preferred_element_type=f32)


def face_count(axis):
    size = lax.axis_size(axis)
    return 0 if size == 1 else 1 if size == 2 else 2


def faces_up(axis, swap):
    return lax.rem(lax.axis_index(axis) + swap, 2) == 0


def doubling(axis):
    size = lax.axis_size(axis)
    return size > 1 and size & (size - 1) == 0


def pack_column(packed, axis, tile, cell):
    here = lax.broadcasted_iota(jnp.int32, tile.shape, 1) == cell
    after = lax.rem(cell + 1, tile.shape[1])
    shifts = [jnp.where(faces_up(axis, i), after, cell) for i in range(len(packed))]
    return [jnp.where(here, pltpu.roll(tile, s, 1), p) for p, s in zip(packed, shifts)]


def copy_faces(faces, field, shape, extra):
    _, nx, ny, nz = shape
    slab = ny * nz
    for refs, axis, width, count, last in (
        (faces[0], "gx", slab, 1, (nx - 1) * slab),
        (faces[1], "gy", nz, nx, slab - nz),
    ):
        for i, ref in enumerate(refs):
            at = pl.multiple_of(jnp.where(faces_up(axis, i), last, 0), nz)
            for j in range(count):
                ref[:, j * width : (j + 1) * width] = field[:, pl.ds(at + j * slab, width)]
        if refs and axis in extra:
            refs[0][:, count * width :] = extra[axis]


def pack_symmetric(square, rows):
    n = square.shape[0]
    half = n // 2
    low = square[half:, half:]
    low = jnp.concatenate([low[: half // 2], low[half // 2 :]], axis=1)
    whole = jnp.concatenate([square[:half], low], axis=0)
    return jnp.concatenate([whole[i : i + rows] for i in range(0, whole.shape[0], rows)], axis=1)


def unpack_symmetric(rows):
    n = rows.shape[1]
    half = n // 2
    low = rows[half:]
    low = jnp.concatenate([low[:, :half], low[:, half:]], axis=0)
    corner = rows[:half, half:]
    return jnp.concatenate([rows[:half], jnp.concatenate([corner.T, low], axis=1)], axis=0)


def pack_square(square, lanes):
    rows = square.shape[0] ** 2 // lanes
    return jnp.concatenate([square[i : i + rows] for i in range(0, square.shape[0], rows)], axis=1)


def unpack_square(rows, n):
    return jnp.concatenate([rows[:, i : i + n] for i in range(0, rows.shape[1], n)], axis=0)


def face_shapes(shape, extra=(), width=0):
    ns, nx, ny, nz = shape
    out = []
    for axis, lanes in (("gx", ny * nz), ("gy", nx * nz), ("gz", nz)):
        n = face_count(axis)
        out.append([(ns, lanes + (width if i == 0 and axis in extra else 0)) for i in range(n)])
    return out


def unflatten(flat):
    out = []
    for axis in ("gx", "gy", "gz"):
        n = face_count(axis)
        out.append(list(flat[:n]))
        flat = flat[n:]
    return out, flat


def exchange(faces):
    got = {}
    for axis, sent in reversed(list(zip(("gx", "gy", "gz"), faces, strict=True))):
        size = lax.axis_size(axis)
        got[axis] = []
        for i, face in enumerate(sent):
            pairs = [(j, j + 1) for j in range(i, size - 1, 2)]
            pairs = pairs + [(j, i) for i, j in pairs]
            got[axis].append(lax.ppermute(face, axis, pairs))
    return [got["gx"], got["gy"], got["gz"]]


def start_kernel(shape, nk, reduced, basis, fine, out_a, out_b, out_bb, *rest):
    ns, nx, ny, nz = shape
    faces, scratch = unflatten(rest)
    r_buf, b_buf, f_buf, rows, both, r_sem, b_sem, f_sem, o_sem = scratch
    slab_at = lambda x: pl.ds(pl.multiple_of(x * ny * nz, ny * nz), ny * nz)
    o_copy = lambda x: pltpu.make_async_copy(both.at[:, slab_at(x)], out_b.at[:, slab_at(x)], o_sem.at[x])
    r_copy = pltpu.make_async_copy(reduced, r_buf, r_sem)
    f_copy = pltpu.make_async_copy(fine, f_buf, f_sem)
    b_copy = lambda x: pltpu.make_async_copy(basis.at[:, x], b_buf.at[x], b_sem.at[x])
    r_copy.start()
    b_copy(0).start()
    f_copy.start()
    for x in range(1, nx):
        b_copy(x).start()
    r_copy.wait()
    r_high, r_low = split(r_buf[...])
    r_twice = jnp.concatenate([r_high, r_high], axis=1)
    group = max(1, min(ny, 256 // nz))

    def body(x, packed):
        b_copy(x).wait()

        @pl.when(x == 0)
        def _():
            f_copy.wait()

        flat = b_buf.at[x].reshape(nk * ny, nz)
        rows[...] = f_buf[:, pl.ds(x, 1)].reshape(ns * ny, nz).astype(f32)
        for y in range(0, ny, group):
            at = pl.multiple_of(x * ny * nz, ny * nz) + y * nz
            parts = [split(flat[pl.ds(y + i, nk, stride=ny), :]) for i in range(group)]
            high = jnp.concatenate([p[0] for p in parts], axis=1)
            low = jnp.concatenate([p[1] for p in parts], axis=1)
            both[:nk, pl.ds(at, group * nz)] = high
            both[nk:, pl.ds(at, group * nz)] = low
            slab = mm(r_twice, jnp.concatenate([high, low], axis=0)) + mm(r_low, high)
            for i in range(group):
                tile = slab[:, i * nz : (i + 1) * nz] + rows[pl.ds(y + i, ns, stride=ny), :]
                out_a[:, pl.ds(at + i * nz, nz)] = tile
                packed = pack_column(packed, "gz", tile, x * ny + y + i)
        o_copy(x).start()
        return packed

    packed = lax.fori_loop(0, nx, body, [jnp.zeros((ns, nz), f32) for _ in faces[2]])
    for ref, value in zip(faces[2], packed):
        ref[...] = value
    product = mm_nt(both[:nk, :], both[...])
    mixed = product[:, nk:]
    out_bb[...] = pack_symmetric(product[:, :nk] + mixed + mixed.T, ns)
    copy_faces(faces, out_a, shape, {"gy": out_bb[...]} if doubling("gy") else {})
    for x in range(nx):
        o_copy(x).wait()


def start(reduced, basis, fine):
    nk = basis.shape[0]
    ns, nx, ny, nz = shape = fine.shape
    width = nk * nk * 3 // 4 // ns
    groups = [s for g in face_shapes(shape, ["gy"] if doubling("gy") else [], width) for s in g]
    outs = pl.pallas_call(
        functools.partial(start_kernel, shape, nk),
        in_specs=[pl.BlockSpec(memory_space=pltpu.HBM)] * 3,
        out_specs=[
            pl.BlockSpec(memory_space=pltpu.HBM if i == 1 else pltpu.VMEM)
            for i in range(3 + len(groups))
        ],
        out_shape=[
            jax.ShapeDtypeStruct((ns, nx * ny * nz), f32),
            pltpu.HBM((2 * nk, nx * ny * nz), bf16),
            jax.ShapeDtypeStruct((ns, width), f32),
        ]
        + [jax.ShapeDtypeStruct(s, f32) for s in groups],
        scratch_shapes=[
            pltpu.VMEM((ns, nk), f32),
            pltpu.VMEM((nx, nk, ny, nz), f32),
            pltpu.VMEM((ns, nx, ny, nz), bf16),
            pltpu.VMEM((ns * ny, nz), f32),
            pltpu.VMEM((2 * nk, nx * ny * nz), bf16),
            pltpu.SemaphoreType.DMA,
            pltpu.SemaphoreType.DMA((nx,)),
            pltpu.SemaphoreType.DMA,
            pltpu.SemaphoreType.DMA((nx,)),
        ],
        compiler_params=pltpu.CompilerParams(vmem_limit_bytes=vmem_limit),
        name="start",
    )(*[pltpu.with_memory_space_constraint(a, pltpu.HBM) for a in (reduced, basis, fine)])
    faces, _ = unflatten(outs[3:])
    return outs[:3], faces


def beside_of(got, axis, before):
    if len(got) == 1:
        return got[0][...]
    return jnp.where(faces_up(axis, 1 if before else 0), got[1][...], got[0][...])


def stencil(shape, x, pad, y_got, z_got, bound_tile, store, args):
    velocity, zone_labels, capacity, rates = args
    ns, nx, ny, nz = shape
    first = {a: lax.axis_index(a) == 0 for a in ("gy", "gz")}
    last = {a: lax.axis_index(a) == lax.axis_size(a) - 1 for a in ("gy", "gz")}
    labels = zone_labels[x]
    cap_slab = jnp.zeros(labels.shape, f32)
    for zone in range(capacity.shape[0]):
        cap_slab = cap_slab + jnp.where(labels == zone + 1, capacity[zone], 0.0)
    surface_slab = jnp.where(cap_slab > 0.0, 1.0, 0.0)
    velocity_slab = velocity[x]
    on = jnp.broadcast_to(rates[:, 0:1], (ns, nz))
    off = jnp.broadcast_to(rates[:, 1:2], (ns, nz))
    lane = lax.broadcasted_iota(jnp.int32, (ns, nz), 1)
    x_at = pl.multiple_of(x * nz, nz)
    y_at = [ref.at[:, pl.ds(x_at, nz)] for ref in y_got]
    left, right = lane == 0, lane == nz - 1
    inner = lane == jnp.where(first["gz"], nz - 1, 0)
    inner_low = lane == jnp.where(first["gz"], -1, 0)
    inner_high = lane == jnp.where(last["gz"], -1, nz - 1)
    for y in range(ny):
        at = pl.multiple_of(x * ny * nz, nz) + y * nz
        tile = lambda slabs_on, rows_on: pad[
            :, pl.ds(pl.multiple_of(at + (slabs_on * ny + rows_on) * nz, nz), nz)
        ]
        centre, behind, ahead = tile(1, 0), tile(0, 0), tile(2, 0)
        if y > 0:
            y_low = tile(1, -1)
        elif y_got:
            y_low = jnp.where(first["gy"], centre, beside_of(y_at, "gy", True))
        else:
            y_low = centre
        if y < ny - 1:
            y_high = tile(1, 1)
        elif y_got:
            y_high = jnp.where(last["gy"], centre, beside_of(y_at, "gy", False))
        else:
            y_high = centre
        z_low, z_high = pltpu.roll(centre, 1, 1), pltpu.roll(centre, nz - 1, 1)
        cell = x * ny + y
        edge = centre
        if len(z_got) == 1:
            shift = jnp.where(first["gz"], nz - 1 - cell, lax.rem(nz - cell, nz))
            edge = jnp.where(inner, pltpu.roll(z_got[0][...], shift, 1), edge)
        elif len(z_got) == 2:
            beside = pltpu.roll(beside_of(z_got, "gz", True), lax.rem(nz - cell, nz), 1)
            edge = jnp.where(inner_low, beside, edge)
            beside = pltpu.roll(beside_of(z_got, "gz", False), nz - 1 - cell, 1)
            edge = jnp.where(inner_high, beside, edge)
        z_low = jnp.where(left, edge, z_low)
        z_high = jnp.where(right, edge, z_high)
        near = behind + ahead + y_low + y_high + z_low + z_high
        row = lambda slab: jnp.broadcast_to(slab[y : y + 1], (ns, nz))
        bound_now = bound_tile(cell, at)
        reaction = row(surface_slab) * (
            on * centre * (row(cap_slab) - bound_now) - off * bound_now
        )
        moved = (
            centre
            + diffusion_number * (near - 6.0 * centre)
            - row(velocity_slab) * (centre - behind)
            - reaction
        )
        store(cell, at, moved, bound_now + reaction)


def fill_pad(shape, pad, analyte, x_got, rates):
    ns, nx, ny, nz = shape
    slab = ny * nz
    pad[:, slab : (nx + 1) * slab] = analyte[...]
    end = (nx + 1) * slab
    for i, ref in enumerate(x_got):
        at = pl.multiple_of(jnp.where(faces_up("gx", i), end, 0), slab)
        pad[:, pl.ds(at, slab)] = ref[:, :slab]

    @pl.when(lax.axis_index("gx") == 0)
    def _():
        pad[:, :slab] = jnp.broadcast_to(rates[:, 2:3], (ns, slab))

    @pl.when(lax.axis_index("gx") == lax.axis_size("gx") - 1)
    def _():
        pad[:, end:] = analyte[:, (nx - 1) * slab :]


def first_kernel(shape, analyte, bound, velocity, zone_labels, capacity, rates, bb, *rest):
    ns, nx, ny, nz = shape
    got, rest = unflatten(rest)
    out_a, out_bound, out_bb = rest[:3]
    faces, (pad,) = unflatten(rest[3:])
    fill_pad(shape, pad, analyte, got[0], rates)

    def body(x, packed):
        packs = [packed]

        def bound_tile(cell, at):
            return bound[pl.ds(cell, ns, stride=nx * ny), :]

        def store(cell, at, moved, bound_then):
            out_bound[:, pl.ds(at, nz)] = bound_then
            out_a[:, pl.ds(at, nz)] = moved
            packs[0] = pack_column(packs[0], "gz", moved, cell)

        stencil(
            shape, x, pad, got[1], got[2], bound_tile, store, (velocity, zone_labels, capacity, rates)
        )
        return packs[0]

    packed = lax.fori_loop(0, nx, body, [jnp.zeros((ns, nz), f32) for _ in faces[2]])
    for ref, value in zip(faces[2], packed):
        ref[...] = value
    out_bb[...] = bb[...] + got[1][0][:, nx * nz :] if doubling("gy") else bb[...]
    copy_faces(faces, out_a, shape, {"gx": out_bb[...]} if doubling("gx") else {})


def second_kernel(shape, nk, analyte, bound, velocity, zone_labels, capacity, rates, bb, both, *rest):
    ns, nx, ny, nz = shape
    got, rest = unflatten(rest)
    out_s, out_bound, out_totals, out_bb, pad, bound_buf, both_buf, sem, both_sem = rest
    both_copy = pltpu.make_async_copy(both, both_buf, both_sem)
    both_copy.start()
    fill_pad(shape, pad, analyte, got[0], rates)

    def body(x, carry):
        def bound_tile(cell, at):
            return bound[:, pl.ds(at, nz)]

        def store(cell, at, moved, bound_then):
            bound_buf[pl.ds(cell, ns, stride=nx * ny), :] = bound_then
            high, low = split(moved)
            out_s[:ns, pl.ds(at, nz)] = high
            out_s[ns:, pl.ds(at, nz)] = low

        stencil(
            shape, x, pad, got[1], got[2], bound_tile, store, (velocity, zone_labels, capacity, rates)
        )
        return carry

    lax.fori_loop(0, nx, body, 0)
    copy = pltpu.make_async_copy(bound_buf, out_bound, sem)
    copy.start()
    snap = out_s[...]
    both_copy.wait()
    product = mm_nt(snap, both_buf[...])
    out_totals[:ns, :] = product[:ns, :nk] + product[:ns, nk:] + product[ns:, :nk]
    square = mm_nt(snap, snap)
    square = square[:ns, :ns] + square[:ns, ns:] + square[ns:, :ns]
    out_totals[ns:, :] = pack_square(square, nk)
    total = bb[...] + got[0][0][:, ny * nz :] if doubling("gx") else bb[...]
    for i in range(total.shape[1] // nk):
        out_bb[i * ns : (i + 1) * ns, :] = total[:, i * nk : (i + 1) * nk]
    copy.wait()


def step_call(kernel, shape, operands, got, out_shape, name, hbm=(), scratch=()):
    ns, nx, ny, nz = shape
    space = {4: pltpu.SMEM, 7: pltpu.HBM if scratch else pltpu.VMEM}
    flat = [g for group in got for g in group]
    in_specs = [
        pl.BlockSpec(memory_space=space.get(i, pltpu.VMEM))
        for i in range(len(operands) + len(flat))
    ]
    return pl.pallas_call(
        kernel,
        in_specs=in_specs,
        out_specs=[
            pl.BlockSpec(memory_space=pltpu.HBM if i in hbm else pltpu.VMEM)
            for i in range(len(out_shape))
        ],
        out_shape=out_shape,
        scratch_shapes=[pltpu.VMEM((ns, (nx + 2) * ny * nz), f32), *scratch],
        compiler_params=pltpu.CompilerParams(vmem_limit_bytes=vmem_limit),
        name=name,
    )(*operands, *flat)


def eliminate(gram, width, between):
    n = gram.shape[0]
    sub = lax.broadcasted_iota(jnp.int32, (n, 2 * n), 0)
    lane = lax.broadcasted_iota(jnp.int32, (n, 2 * n), 1)
    unit = jnp.where(sub[:, :n] == lane[:, :n], 1.0, 0.0)
    work = jnp.concatenate([gram, unit], axis=1)
    for start_at in range(0, n, width):
        columns = [
            jnp.broadcast_to(work[:, start_at + i : start_at + i + 1], (n, 2 * n))
            for i in range(width)
        ]
        for i in range(width):
            j = start_at + i
            scale = jnp.where(sub > j, columns[i] / columns[i][j : j + 1, :], 0.0)
            for k in range(i + 1, width):
                columns[k] = columns[k] - scale * columns[k][j : j + 1, :]
            work = work - scale * work[j : j + 1, :]
            between(j)
    pivots = jnp.sum(jnp.where(lane == sub, work, 0.0), axis=1, keepdims=True)
    work = work / jnp.sqrt(pivots)
    return jnp.where(lane[:, :n] >= sub[:, :n], work[:, :n], 0.0), work[:, n:]


def finish_kernel(shape, nk, inverse_rows, totals, snap, both, out_modes, out_factor, out_coeffs, *scratch):
    ns, nx, ny, nz = shape
    slab = ny * nz
    rest, modes, both_buf, sem, both_sem = scratch
    part = lambda x: slice(x * slab, (x + 1) * slab)
    both_copy = lambda x: pltpu.make_async_copy(both.at[:, part(x)], both_buf.at[:, part(x)], both_sem.at[x])
    for x in range(nx):
        both_copy(x).start()
    coeffs = totals[:ns, :] * inverse_rows
    out_coeffs[...] = coeffs
    c_high, c_low = split(coeffs)
    c_twice = jnp.concatenate([c_high, c_high], axis=1)
    squares = ns + ns * ns // nk
    weighted = mm_exact(coeffs, unpack_symmetric(totals[squares:, :] * inverse_rows))
    exact_nt = functools.partial(
        lax.dot_general,
        dimension_numbers=(((1,), (1,)), ((), ())),
        precision=highest,
        preferred_element_type=f32,
    )
    mixed = exact_nt(coeffs, coeffs)
    gram = unpack_square(totals[ns:squares, :] * inverse_rows, ns) - mixed - mixed + exact_nt(weighted, coeffs)

    pieces = 2 * nx if ny % 2 == 0 and 2 * nx <= ns else nx
    width = nx * slab // pieces

    def residual(j):
        if j >= pieces:
            return
        if j % (pieces // nx) == 0:
            both_copy(j // (pieces // nx)).wait()
        at = slice(j * width, (j + 1) * width)
        value = snap[:ns, at].astype(f32) + snap[ns:, at].astype(f32)
        value = value - (mm(c_twice, both_buf[:, at]) + mm(c_low, both_buf[:nk, at]))
        high, low = split(value)
        rest[:ns, at] = high
        rest[ns:, at] = low

    factor, inverse = eliminate(gram, 8 if ns % 8 == 0 else 1, residual)
    out_factor[...] = factor
    i_high, i_low = split(inverse)
    i_twice = jnp.concatenate([i_high, i_high], axis=1)
    copy = lambda x: pltpu.make_async_copy(modes.at[:, x], out_modes.at[:, x], sem.at[x])
    flat = modes.reshape(ns * nx * ny, nz)
    for x in range(nx):
        at = slice(x * slab, (x + 1) * slab)
        value = mm(i_twice, rest[:, at]) + mm(i_low, rest[:ns, at])
        for y in range(ny):
            flat[pl.ds(x * ny + y, ns, stride=nx * ny), :] = value[:, y * nz : (y + 1) * nz]
        copy(x).start()
    for x in range(nx):
        copy(x).wait()


def finish(shape, inverse_rows, totals, snap, both):
    ns, nx, ny, nz = shape
    nk = both.shape[0] // 2
    vmem = pl.BlockSpec(memory_space=pltpu.VMEM)
    return pl.pallas_call(
        functools.partial(finish_kernel, shape, nk, inverse_rows),
        in_specs=[vmem, vmem, pl.BlockSpec(memory_space=pltpu.HBM)],
        out_specs=[pl.BlockSpec(memory_space=pltpu.HBM), vmem, vmem],
        out_shape=[
            jax.ShapeDtypeStruct(shape, f32),
            jax.ShapeDtypeStruct((ns, ns), f32),
            jax.ShapeDtypeStruct((ns, nk), f32),
        ],
        scratch_shapes=[
            pltpu.VMEM((2 * ns, nx * ny * nz), bf16),
            pltpu.VMEM(shape, f32),
            pltpu.VMEM(both.shape, bf16),
            pltpu.SemaphoreType.DMA((nx,)),
            pltpu.SemaphoreType.DMA((nx,)),
        ],
        compiler_params=pltpu.CompilerParams(vmem_limit_bytes=vmem_limit),
        name="finish",
    )(totals, snap, both)


def sum_over(small, large):
    def swapped(value, axis, stride):
        size = lax.axis_size(axis)
        return value + lax.ppermute(value, axis, [(i, i ^ stride) for i in range(size)])

    for axis in ("gy", "gx"):
        if doubling(axis):
            small = swapped(small, axis, 1)
    value = jnp.concatenate([small, large], axis=0)
    for axis in ("gz", "gy", "gx"):
        size = lax.axis_size(axis)
        if not doubling(axis):
            value = lax.psum(value, axis) if size > 1 else value
            continue
        stride = 1 if axis == "gz" else 2
        while stride < size:
            value = swapped(value, axis, stride)
            stride *= 2
    return value


def on_device(
    basis_modes,
    reduced_state,
    fine_state,
    bound_state,
    velocity,
    zone_labels,
    capacity,
    on_rate,
    off_rate,
    inlet_level,
):
    ns, nx, ny, nz = shape = fine_state.shape
    nk = basis_modes.shape[0]
    cells = nx * ny * nz
    rates = jnp.stack([on_rate, off_rate, inlet_level], axis=1)
    (analyte, both, bb), faces = start(reduced_state.T, basis_modes, fine_state)
    got = exchange(faces)
    both = pltpu.with_memory_space_constraint(both, pltpu.HBM)
    fields = [velocity, zone_labels, capacity, rates]
    struct = jax.ShapeDtypeStruct
    outs = step_call(
        functools.partial(first_kernel, shape),
        shape,
        [analyte, bound_state.reshape(ns * nx * ny, nz)] + fields + [bb],
        got,
        [struct((ns, cells), f32), struct((ns, cells), f32), struct(bb.shape, f32)]
        + [
            struct(s, f32)
            for g in face_shapes(shape, ["gx"] if doubling("gx") else [], bb.shape[1])
            for s in g
        ],
        "first_step",
    )
    faces, _ = unflatten(outs[3:])
    got = exchange(faces)
    snap, bound_next, small, large = step_call(
        functools.partial(second_kernel, shape, nk),
        shape,
        [outs[0], outs[1]] + fields + [outs[2], both],
        got,
        [
            struct((2 * ns, cells), bf16),
            struct((ns * nx * ny, nz), f32),
            struct((ns + ns * ns // nk, nk), f32),
            struct((bb.size // nk, nk), f32),
        ],
        "second_step",
        hbm=(1,),
        scratch=[
            pltpu.VMEM((ns * nx * ny, nz), f32),
            pltpu.VMEM((2 * nk, cells), bf16),
            pltpu.SemaphoreType.DMA,
            pltpu.SemaphoreType.DMA,
        ],
    )
    totals = sum_over(small, large)
    inverse_rows = 1.0 / (
        cells * lax.axis_size("gx") * lax.axis_size("gy") * lax.axis_size("gz")
    )
    modes, factor, coeffs = finish(shape, inverse_rows, totals, snap, both)
    return (modes, factor, coeffs.T, bound_next.reshape(shape))


def solution(mesh):
    return jax.shard_map(
        on_device,
        mesh=mesh,
        in_specs=(
            P(None, ("grp", "gx"), "gy", "gz"),
            P("grp", None),
            P(None, ("grp", "gx"), "gy", "gz"),
            P(None, ("grp", "gx"), "gy", "gz"),
            P(("grp", "gx"), "gy", "gz"),
            P(("grp", "gx"), "gy", "gz"),
            P(),
            P(),
            P(),
            P("grp"),
        ),
        out_specs=(
            P(None, ("grp", "gx"), "gy", "gz"),
            P("grp", None),
            P("grp", None),
            P(None, ("grp", "gx"), "gy", "gz"),
        ),
        check_vma=False,
    )
```

```python
import functools

import jax
import jax.numpy as jnp
from jax import lax
from jax.experimental import pallas as pl
from jax.experimental.pallas import tpu as pltpu
from jax.sharding import PartitionSpec as P

highest = lax.Precision.HIGHEST
diffusion_number = 0.03
f32 = jnp.float32
bf16 = jnp.bfloat16
vmem_limit = 16 << 20


def split(value):
    high = value.astype(bf16)
    return high, (value - high.astype(f32)).astype(bf16)


def mm(a, b):
    return jnp.dot(a, b, preferred_element_type=f32)


def mm_nt(a, b):
    return lax.dot_general(a, b, (((1,), (1,)), ((), ())), preferred_element_type=f32)


def mm_exact(a, b):
    return jnp.dot(a, b, precision=highest, preferred_element_type=f32)


def face_count(axis):
    size = lax.axis_size(axis)
    return 0 if size == 1 else 1 if size == 2 else 2


def faces_up(axis, swap):
    return lax.rem(lax.axis_index(axis) + swap, 2) == 0


def doubling(axis):
    size = lax.axis_size(axis)
    return size > 1 and size & (size - 1) == 0


def pack_column(packed, axis, tile, cell):
    here = lax.broadcasted_iota(jnp.int32, tile.shape, 1) == cell
    after = lax.rem(cell + 1, tile.shape[1])
    shifts = [jnp.where(faces_up(axis, i), after, cell) for i in range(len(packed))]
    return [jnp.where(here, pltpu.roll(tile, s, 1), p) for p, s in zip(packed, shifts)]


def copy_faces(faces, field, shape, extra):
    _, nx, ny, nz = shape
    slab = ny * nz
    for refs, axis, width, count, last in (
        (faces[0], "gx", slab, 1, (nx - 1) * slab),
        (faces[1], "gy", nz, nx, slab - nz),
    ):
        for i, ref in enumerate(refs):
            at = pl.multiple_of(jnp.where(faces_up(axis, i), last, 0), nz)
            for j in range(count):
                ref[:, j * width : (j + 1) * width] = field[:, pl.ds(at + j * slab, width)]
        if refs and axis in extra:
            refs[0][:, count * width :] = extra[axis]


def pack_symmetric(square, rows):
    n = square.shape[0]
    half = n // 2
    low = square[half:, half:]
    low = jnp.concatenate([low[: half // 2], low[half // 2 :]], axis=1)
    whole = jnp.concatenate([square[:half], low], axis=0)
    return jnp.concatenate([whole[i : i + rows] for i in range(0, whole.shape[0], rows)], axis=1)


def unpack_symmetric(rows):
    n = rows.shape[1]
    half = n // 2
    low = rows[half:]
    low = jnp.concatenate([low[:, :half], low[:, half:]], axis=0)
    corner = rows[:half, half:]
    return jnp.concatenate([rows[:half], jnp.concatenate([corner.T, low], axis=1)], axis=0)


def pack_square(square, lanes):
    rows = square.shape[0] ** 2 // lanes
    return jnp.concatenate([square[i : i + rows] for i in range(0, square.shape[0], rows)], axis=1)


def unpack_square(rows, n):
    return jnp.concatenate([rows[:, i : i + n] for i in range(0, rows.shape[1], n)], axis=0)


def face_shapes(shape, extra=(), width=0):
    ns, nx, ny, nz = shape
    out = []
    for axis, lanes in (("gx", ny * nz), ("gy", nx * nz), ("gz", nz)):
        n = face_count(axis)
        out.append([(ns, lanes + (width if i == 0 and axis in extra else 0)) for i in range(n)])
    return out


def unflatten(flat):
    out = []
    for axis in ("gx", "gy", "gz"):
        n = face_count(axis)
        out.append(list(flat[:n]))
        flat = flat[n:]
    return out, flat


def exchange(faces):
    got = {}
    for axis, sent in reversed(list(zip(("gx", "gy", "gz"), faces, strict=True))):
        size = lax.axis_size(axis)
        got[axis] = []
        for i, face in enumerate(sent):
            pairs = [(j, j + 1) for j in range(i, size - 1, 2)]
            pairs = pairs + [(j, i) for i, j in pairs]
            got[axis].append(lax.ppermute(face, axis, pairs))
    return [got["gx"], got["gy"], got["gz"]]


def start_kernel(shape, nk, reduced, basis, fine, bound, on, off, inlet, out_a, out_bb, out_bound, out_rates, *rest):
    ns, nx, ny, nz = shape
    both, rest = rest[:nx], rest[nx:]
    faces, scratch = unflatten(rest)
    r_buf, b_buf, f_buf, rows, on_buf, off_buf, inlet_buf, r_sem, b_sem, f_sem, bound_sem, rate_sem = scratch
    rate_bufs = (on_buf, off_buf, inlet_buf)
    rate_copies = [
        pltpu.make_async_copy(a, b, rate_sem.at[i])
        for i, (a, b) in enumerate(zip((on, off, inlet), rate_bufs))
    ]
    bound_copy = lambda x: pltpu.make_async_copy(bound.at[:, x], out_bound.at[x], bound_sem.at[x])
    r_copy = pltpu.make_async_copy(reduced, r_buf, r_sem)
    f_copy = pltpu.make_async_copy(fine, f_buf, f_sem)
    b_copy = lambda x: pltpu.make_async_copy(basis.at[:, x], b_buf.at[x], b_sem.at[x])
    r_copy.start()
    b_copy(0).start()
    f_copy.start()
    for x in range(1, nx):
        b_copy(x).start()
    for copy in rate_copies:
        copy.start()
    for x in range(nx):
        bound_copy(x).start()
    r_copy.wait()
    r_high, r_low = split(r_buf[...])
    r_twice = jnp.concatenate([r_high, r_high], axis=1)
    for copy in rate_copies:
        copy.wait()
    lane = lax.broadcasted_iota(jnp.int32, (ns, ns), 1)
    own = lax.broadcasted_iota(jnp.int32, (ns, ns), 0) == lane
    column = lambda ref: jnp.sum(
        jnp.where(own, jnp.broadcast_to(ref[...], (ns, ns)), 0.0), axis=1, keepdims=True
    )
    lane = lax.broadcasted_iota(jnp.int32, out_rates.shape, 1)
    out_rates[...] = jnp.where(
        lane == 0, column(on_buf), jnp.where(lane == 1, column(off_buf), column(inlet_buf))
    )
    group = max(1, min(ny, 256 // nz))

    def body(x, packed):
        b_copy(x).wait()

        if x == 0:
            f_copy.wait()
        flat = b_buf.at[x].reshape(nk * ny, nz)
        rows[...] = f_buf[:, pl.ds(x, 1)].reshape(ns * ny, nz).astype(f32)
        for y in range(0, ny, group):
            at = (x * ny + y) * nz
            parts = [split(flat[pl.ds(y + i, nk, stride=ny), :]) for i in range(group)]
            high = jnp.concatenate([p[0] for p in parts], axis=1)
            low = jnp.concatenate([p[1] for p in parts], axis=1)
            both[x][:nk, pl.ds(y * nz, group * nz)] = high
            both[x][nk:, pl.ds(y * nz, group * nz)] = low
            slab = mm(r_twice, jnp.concatenate([high, low], axis=0)) + mm(r_low, high)
            for i in range(group):
                tile = slab[:, i * nz : (i + 1) * nz] + rows[pl.ds(y + i, ns, stride=ny), :]
                out_a[:, pl.ds(at + i * nz, nz)] = tile
                packed = pack_column(packed, "gz", tile, x * ny + y + i)
        return packed

    packed = [jnp.zeros((ns, nz), f32) for _ in faces[2]]
    for x in range(nx):
        packed = body(x, packed)
    for ref, value in zip(faces[2], packed):
        ref[...] = value
    product = sum(mm_nt(piece[:nk, :], piece[...]) for piece in both)
    mixed = product[:, nk:]
    out_bb[...] = pack_symmetric(product[:, :nk] + mixed + mixed.T, ns)
    copy_faces(faces, out_a, shape, {"gy": out_bb[...]} if doubling("gy") else {})
    for x in range(nx):
        bound_copy(x).wait()


def start(reduced, basis, fine, bound, rates):
    nk = basis.shape[0]
    ns, nx, ny, nz = shape = fine.shape
    width = nk * nk * 3 // 4 // ns
    groups = [s for g in face_shapes(shape, ["gy"] if doubling("gy") else [], width) for s in g]
    outs = pl.pallas_call(
        functools.partial(start_kernel, shape, nk),
        in_specs=[pl.BlockSpec(memory_space=pltpu.HBM)] * 7,
        out_specs=[
            pl.BlockSpec(memory_space=pltpu.VMEM) for _ in range(4 + nx + len(groups))
        ],
        out_shape=[
            jax.ShapeDtypeStruct((ns, nx * ny * nz), f32),
            jax.ShapeDtypeStruct((ns, width), f32),
            jax.ShapeDtypeStruct((nx, ns, ny, nz), f32),
            jax.ShapeDtypeStruct((ns, nz), f32),
        ]
        + [jax.ShapeDtypeStruct((2 * nk, ny * nz), bf16)] * nx
        + [jax.ShapeDtypeStruct(s, f32) for s in groups],
        scratch_shapes=[
            pltpu.VMEM((ns, nk), f32),
            pltpu.VMEM((nx, nk, ny, nz), f32),
            pltpu.VMEM((ns, nx, ny, nz), bf16),
            pltpu.VMEM((ns * ny, nz), f32),
            pltpu.VMEM((1, ns), f32),
            pltpu.VMEM((1, ns), f32),
            pltpu.VMEM((1, ns), f32),
            pltpu.SemaphoreType.DMA,
            pltpu.SemaphoreType.DMA((nx,)),
            pltpu.SemaphoreType.DMA,
            pltpu.SemaphoreType.DMA((nx,)),
            pltpu.SemaphoreType.DMA((3,)),
        ],
        compiler_params=pltpu.CompilerParams(vmem_limit_bytes=vmem_limit),
        name="start",
    )(*[pltpu.with_memory_space_constraint(a, pltpu.HBM) for a in (reduced, basis, fine, bound, *rates)])
    faces, _ = unflatten(outs[4 + nx :])
    return outs[:4], outs[4 : 4 + nx], faces


def beside_of(got, axis, before):
    if len(got) == 1:
        return got[0][...]
    return jnp.where(faces_up(axis, 1 if before else 0), got[1][...], got[0][...])


def stencil(shape, x, pad, y_got, z_got, bound_tile, store, args):
    velocity, zone_labels, capacity, rates = args
    ns, nx, ny, nz = shape
    first = {a: lax.axis_index(a) == 0 for a in ("gy", "gz")}
    last = {a: lax.axis_index(a) == lax.axis_size(a) - 1 for a in ("gy", "gz")}
    labels = zone_labels[x]
    cap_slab = jnp.zeros(labels.shape, f32)
    for zone in range(capacity.shape[0]):
        cap_slab = cap_slab + jnp.where(labels == zone + 1, capacity[zone], 0.0)
    surface_slab = jnp.where(cap_slab > 0.0, 1.0, 0.0)
    velocity_slab = velocity[x]
    on = jnp.broadcast_to(rates[:, 0:1], (ns, nz))
    off = jnp.broadcast_to(rates[:, 1:2], (ns, nz))
    lane = lax.broadcasted_iota(jnp.int32, (ns, nz), 1)
    x_at = pl.multiple_of(x * nz, nz)
    y_at = [ref.at[:, pl.ds(x_at, nz)] for ref in y_got]
    left, right = lane == 0, lane == nz - 1
    inner = lane == jnp.where(first["gz"], nz - 1, 0)
    inner_low = lane == jnp.where(first["gz"], -1, 0)
    inner_high = lane == jnp.where(last["gz"], -1, nz - 1)
    for y in range(ny):
        at = pl.multiple_of(x * ny * nz, nz) + y * nz
        tile = lambda slabs_on, rows_on: pad[
            :, pl.ds(pl.multiple_of(at + (slabs_on * ny + rows_on) * nz, nz), nz)
        ]
        centre, behind, ahead = tile(1, 0), tile(0, 0), tile(2, 0)
        if y > 0:
            y_low = tile(1, -1)
        elif y_got:
            y_low = jnp.where(first["gy"], centre, beside_of(y_at, "gy", True))
        else:
            y_low = centre
        if y < ny - 1:
            y_high = tile(1, 1)
        elif y_got:
            y_high = jnp.where(last["gy"], centre, beside_of(y_at, "gy", False))
        else:
            y_high = centre
        z_low, z_high = pltpu.roll(centre, 1, 1), pltpu.roll(centre, nz - 1, 1)
        cell = x * ny + y
        edge = centre
        if len(z_got) == 1:
            shift = jnp.where(first["gz"], nz - 1 - cell, lax.rem(nz - cell, nz))
            edge = jnp.where(inner, pltpu.roll(z_got[0][...], shift, 1), edge)
        elif len(z_got) == 2:
            beside = pltpu.roll(beside_of(z_got, "gz", True), lax.rem(nz - cell, nz), 1)
            edge = jnp.where(inner_low, beside, edge)
            beside = pltpu.roll(beside_of(z_got, "gz", False), nz - 1 - cell, 1)
            edge = jnp.where(inner_high, beside, edge)
        z_low = jnp.where(left, edge, z_low)
        z_high = jnp.where(right, edge, z_high)
        near = behind + ahead + y_low + y_high + z_low + z_high
        row = lambda slab: jnp.broadcast_to(slab[y : y + 1], (ns, nz))
        bound_now = bound_tile(y, at)
        reaction = row(surface_slab) * (
            on * centre * (row(cap_slab) - bound_now) - off * bound_now
        )
        moved = (
            centre
            + diffusion_number * (near - 6.0 * centre)
            - row(velocity_slab) * (centre - behind)
            - reaction
        )
        store(cell, y, at, moved, bound_now + reaction)


def fill_pad(shape, pad, analyte, x_got, rates):
    ns, nx, ny, nz = shape
    slab = ny * nz
    pad[:, slab : (nx + 1) * slab] = analyte[...]
    end = (nx + 1) * slab
    for i, ref in enumerate(x_got):
        at = pl.multiple_of(jnp.where(faces_up("gx", i), end, 0), slab)
        pad[:, pl.ds(at, slab)] = ref[:, :slab]

    @pl.when(lax.axis_index("gx") == 0)
    def _():
        pad[:, :slab] = jnp.broadcast_to(rates[:, 2:3], (ns, slab))

    @pl.when(lax.axis_index("gx") == lax.axis_size("gx") - 1)
    def _():
        pad[:, end:] = analyte[:, (nx - 1) * slab :]


def first_kernel(shape, analyte, bound, velocity, zone_labels, capacity, rates, bb, *rest):
    ns, nx, ny, nz = shape
    got, rest = unflatten(rest)
    out_a, out_bound, out_bb = rest[:3]
    faces, (pad,) = unflatten(rest[3:])
    fill_pad(shape, pad, analyte, got[0], rates)

    def body(x, packed):
        packs = [packed]

        rows = bound.at[x].reshape(ns * ny, nz)

        def bound_tile(y, at):
            return rows[pl.ds(y, ns, stride=ny), :]

        def store(cell, y, at, moved, bound_then):
            out_bound[:, pl.ds(at, nz)] = bound_then
            out_a[:, pl.ds(at, nz)] = moved
            packs[0] = pack_column(packs[0], "gz", moved, cell)

        stencil(
            shape, x, pad, got[1], got[2], bound_tile, store, (velocity, zone_labels, capacity, rates)
        )
        return packs[0]

    packed = lax.fori_loop(0, nx, body, [jnp.zeros((ns, nz), f32) for _ in faces[2]])
    for ref, value in zip(faces[2], packed):
        ref[...] = value
    out_bb[...] = bb[...] + got[1][0][:, nx * nz :] if doubling("gy") else bb[...]
    copy_faces(faces, out_a, shape, {"gx": out_bb[...]} if doubling("gx") else {})


def second_kernel(shape, nk, analyte, bound, velocity, zone_labels, capacity, rates, bb, *rest):
    ns, nx, ny, nz = shape
    both, rest = rest[:nx], rest[nx:]
    got, rest = unflatten(rest)
    out_s, out_bound, out_totals, out_bb, pad, bound_buf, sem = rest
    fill_pad(shape, pad, analyte, got[0], rates)

    def body(x, carry):
        rows = bound_buf.at[x].reshape(ns * ny, nz)

        def bound_tile(y, at):
            return bound[:, pl.ds(at, nz)]

        def store(cell, y, at, moved, bound_then):
            rows[pl.ds(y, ns, stride=ny), :] = bound_then
            high, low = split(moved)
            out_s[:ns, pl.ds(at, nz)] = high
            out_s[ns:, pl.ds(at, nz)] = low

        stencil(
            shape, x, pad, got[1], got[2], bound_tile, store, (velocity, zone_labels, capacity, rates)
        )
        copy(x).start()
        return carry

    copy = lambda x: pltpu.make_async_copy(bound_buf.at[x], out_bound.at[:, x], sem.at[x])
    lax.fori_loop(0, nx, body, 0)
    snap = out_s[...]
    slab = ny * nz
    product = sum(mm_nt(out_s[:, x * slab : (x + 1) * slab], both[x][...]) for x in range(nx))
    out_totals[:ns, :] = product[:ns, :nk] + product[:ns, nk:] + product[ns:, :nk]
    square = mm_nt(snap, snap)
    square = square[:ns, :ns] + square[:ns, ns:] + square[ns:, :ns]
    out_totals[ns:, :] = pack_square(square, nk)
    total = bb[...] + got[0][0][:, ny * nz :] if doubling("gx") else bb[...]
    for i in range(total.shape[1] // nk):
        out_bb[i * ns : (i + 1) * ns, :] = total[:, i * nk : (i + 1) * nk]
    for x in range(nx):
        copy(x).wait()


def step_call(kernel, shape, operands, got, out_shape, name, hbm=(), scratch=(), aliases=None):
    ns, nx, ny, nz = shape
    space = {4: pltpu.SMEM}
    flat = [g for group in got for g in group]
    in_specs = [
        pl.BlockSpec(memory_space=space.get(i, pltpu.VMEM))
        for i in range(len(operands) + len(flat))
    ]
    return pl.pallas_call(
        kernel,
        in_specs=in_specs,
        out_specs=[
            pl.BlockSpec(memory_space=pltpu.HBM if i in hbm else pltpu.VMEM)
            for i in range(len(out_shape))
        ],
        out_shape=out_shape,
        scratch_shapes=[pltpu.VMEM((ns, (nx + 2) * ny * nz), f32), *scratch],
        input_output_aliases=aliases or {},
        compiler_params=pltpu.CompilerParams(vmem_limit_bytes=vmem_limit),
        name=name,
    )(*operands, *flat)


def eliminate(gram, width, between):
    n = gram.shape[0]
    sub = lax.broadcasted_iota(jnp.int32, (n, 2 * n), 0)
    lane = lax.broadcasted_iota(jnp.int32, (n, 2 * n), 1)
    unit = jnp.where(sub[:, :n] == lane[:, :n], 1.0, 0.0)
    work = jnp.concatenate([gram, unit], axis=1)
    for start_at in range(0, n, width):
        columns = [
            jnp.broadcast_to(work[:, start_at + i : start_at + i + 1], (n, 2 * n))
            for i in range(width)
        ]
        for i in range(width):
            j = start_at + i
            scale = jnp.where(sub > j, columns[i] / columns[i][j : j + 1, :], 0.0)
            for k in range(i + 1, width):
                columns[k] = columns[k] - scale * columns[k][j : j + 1, :]
            work = work - scale * work[j : j + 1, :]
            between(j)
    pivots = jnp.sum(jnp.where(lane == sub, work, 0.0), axis=1, keepdims=True)
    work = work / jnp.sqrt(pivots)
    return jnp.where(lane[:, :n] >= sub[:, :n], work[:, :n], 0.0), work[:, n:]


def finish_kernel(shape, nk, inverse_rows, totals, snap, *refs):
    ns, nx, ny, nz = shape
    both, (out_modes, out_factor, out_coeffs, *scratch) = refs[:nx], refs[nx:]
    slab = ny * nz
    rest, modes, sem = scratch
    coeffs = totals[:ns, :] * inverse_rows
    out_coeffs[...] = coeffs
    c_high, c_low = split(coeffs)
    c_twice = jnp.concatenate([c_high, c_high], axis=1)
    squares = ns + ns * ns // nk
    weighted = mm_exact(coeffs, unpack_symmetric(totals[squares:, :] * inverse_rows))
    exact_nt = functools.partial(
        lax.dot_general,
        dimension_numbers=(((1,), (1,)), ((), ())),
        precision=highest,
        preferred_element_type=f32,
    )
    mixed = exact_nt(coeffs, coeffs)
    gram = unpack_square(totals[ns:squares, :] * inverse_rows, ns) - mixed - mixed + exact_nt(weighted, coeffs)

    pieces = 2 * nx if ny % 2 == 0 and 2 * nx <= ns else nx
    width = nx * slab // pieces

    def residual(j):
        if j >= pieces:
            return
        at = slice(j * width, (j + 1) * width)
        value = snap[:ns, at].astype(f32) + snap[ns:, at].astype(f32)
        piece = both[at.start // slab]
        on = slice(at.start % slab, at.start % slab + width)
        value = value - (mm(c_twice, piece[:, on]) + mm(c_low, piece[:nk, on]))
        high, low = split(value)
        rest[:ns, at] = high
        rest[ns:, at] = low

    factor, inverse = eliminate(gram, 8 if ns % 8 == 0 else 1, residual)
    out_factor[...] = factor
    i_high, i_low = split(inverse)
    i_twice = jnp.concatenate([i_high, i_high], axis=1)
    copy = lambda x: pltpu.make_async_copy(modes.at[x], out_modes.at[:, x], sem.at[x])
    for x in range(nx):
        at = slice(x * slab, (x + 1) * slab)
        value = mm(i_twice, rest[:, at]) + mm(i_low, rest[:ns, at])
        flat = modes.at[x].reshape(ns * ny, nz)
        for y in range(ny):
            flat[pl.ds(y, ns, stride=ny), :] = value[:, y * nz : (y + 1) * nz]
        copy(x).start()
    for x in range(nx):
        copy(x).wait()


def finish(shape, inverse_rows, totals, snap, both):
    ns, nx, ny, nz = shape
    nk = both[0].shape[0] // 2
    vmem = pl.BlockSpec(memory_space=pltpu.VMEM)
    return pl.pallas_call(
        functools.partial(finish_kernel, shape, nk, inverse_rows),
        in_specs=[vmem] * (2 + nx),
        out_specs=[pl.BlockSpec(memory_space=pltpu.HBM), vmem, vmem],
        out_shape=[
            jax.ShapeDtypeStruct(shape, f32),
            jax.ShapeDtypeStruct((ns, ns), f32),
            jax.ShapeDtypeStruct((ns, nk), f32),
        ],
        scratch_shapes=[
            pltpu.VMEM((2 * ns, nx * ny * nz), bf16),
            pltpu.VMEM((nx, ns, ny, nz), f32),
            pltpu.SemaphoreType.DMA((nx,)),
        ],
        compiler_params=pltpu.CompilerParams(vmem_limit_bytes=vmem_limit),
        name="finish",
    )(totals, snap, *both)


def sum_over(small, large):
    def swapped(value, axis, stride):
        size = lax.axis_size(axis)
        return value + lax.ppermute(value, axis, [(i, i ^ stride) for i in range(size)])

    for axis in ("gy", "gx"):
        if doubling(axis):
            small = swapped(small, axis, 1)
    value = jnp.concatenate([small, large], axis=0)
    for axis in ("gz", "gy", "gx"):
        size = lax.axis_size(axis)
        if not doubling(axis):
            value = lax.psum(value, axis) if size > 1 else value
            continue
        stride = 1 if axis == "gz" else 2
        while stride < size:
            value = swapped(value, axis, stride)
            stride *= 2
    return value


def on_device(
    basis_modes,
    reduced_state,
    fine_state,
    bound_state,
    velocity,
    zone_labels,
    capacity,
    on_rate,
    off_rate,
    inlet_level,
):
    ns, nx, ny, nz = shape = fine_state.shape
    nk = basis_modes.shape[0]
    cells = nx * ny * nz
    rates = [value[None] for value in (on_rate, off_rate, inlet_level)]
    (analyte, bb, bound, rates), both, faces = start(
        reduced_state.T, basis_modes, fine_state, bound_state, rates
    )
    got = exchange(faces)
    fields = [velocity, zone_labels, capacity, rates]
    struct = jax.ShapeDtypeStruct
    outs = step_call(
        functools.partial(first_kernel, shape),
        shape,
        [analyte, bound] + fields + [bb],
        got,
        [struct((ns, cells), f32), struct((ns, cells), f32), struct(bb.shape, f32)]
        + [
            struct(s, f32)
            for g in face_shapes(shape, ["gx"] if doubling("gx") else [], bb.shape[1])
            for s in g
        ],
        "first_step",
    )
    faces, _ = unflatten(outs[3:])
    got = exchange(faces)
    snap, bound_next, small, large = step_call(
        functools.partial(second_kernel, shape, nk),
        shape,
        [outs[0], outs[1]] + fields + [outs[2], *both],
        got,
        [
            struct((2 * ns, cells), bf16),
            struct(shape, f32),
            struct((ns + ns * ns // nk, nk), f32),
            struct((bb.size // nk, nk), f32),
        ],
        "second_step",
        hbm=(1,),
        scratch=[
            pltpu.VMEM((nx, ns, ny, nz), f32),
            pltpu.SemaphoreType.DMA((nx,)),
        ],
    )
    totals = sum_over(small, large)
    inverse_rows = 1.0 / (
        cells * lax.axis_size("gx") * lax.axis_size("gy") * lax.axis_size("gz")
    )
    modes, factor, coeffs = finish(shape, inverse_rows, totals, snap, both)
    return (modes, factor, coeffs.T, bound_next)


def solution(mesh):
    return jax.shard_map(
        on_device,
        mesh=mesh,
        in_specs=(
            P(None, ("grp", "gx"), "gy", "gz"),
            P("grp", None),
            P(None, ("grp", "gx"), "gy", "gz"),
            P(None, ("grp", "gx"), "gy", "gz"),
            P(("grp", "gx"), "gy", "gz"),
            P(("grp", "gx"), "gy", "gz"),
            P(),
            P(),
            P(),
            P("grp"),
        ),
        out_specs=(
            P(None, ("grp", "gx"), "gy", "gz"),
            P("grp", None),
            P("grp", None),
            P(None, ("grp", "gx"), "gy", "gz"),
        ),
        check_vma=False,
    )
```

```python
import functools

import jax
import jax.numpy as jnp
from jax import lax
from jax.experimental import pallas as pl
from jax.experimental.pallas import tpu as pltpu
from jax.sharding import PartitionSpec as P

highest = lax.Precision.HIGHEST
diffusion_number = 0.03
f32 = jnp.float32
bf16 = jnp.bfloat16
vmem_limit = 16 << 20


def split(value):
    high = value.astype(bf16)
    return high, (value - high.astype(f32)).astype(bf16)


def mm(a, b):
    return jnp.dot(a, b, preferred_element_type=f32)


def aligned(offset, size):
    return offset if isinstance(offset, int) else pl.multiple_of(offset, size)


def stacked(high, low):
    low = jnp.concatenate([low, jnp.zeros_like(low)], axis=1)
    return jnp.concatenate([jnp.concatenate([high, high], axis=1), low], axis=0)


def mm_nt(a, b):
    return lax.dot_general(a, b, (((1,), (1,)), ((), ())), preferred_element_type=f32)


def mm_exact(a, b):
    return jnp.dot(a, b, precision=highest, preferred_element_type=f32)


def face_count(axis):
    size = lax.axis_size(axis)
    return 0 if size == 1 else 1 if size == 2 else 2


def faces_up(axis, swap):
    return lax.rem(lax.axis_index(axis) + swap, 2) == 0


def doubling(axis):
    size = lax.axis_size(axis)
    return size > 1 and size & (size - 1) == 0


def pack_column(packed, axis, tile, cell):
    here = lax.broadcasted_iota(jnp.int32, tile.shape, 1) == cell
    after = lax.rem(cell + 1, tile.shape[1])
    shifts = [jnp.where(faces_up(axis, i), after, cell) for i in range(len(packed))]
    return [jnp.where(here, pltpu.roll(tile, s, 1), p) for p, s in zip(packed, shifts)]


def pack_columns(refs, field, shape):
    ns, nx, ny, nz = shape

    def body(x, packed):
        for y in range(ny):
            tile = field[:, pl.ds(pl.multiple_of(x * ny * nz, ny * nz) + y * nz, nz)]
            packed = pack_column(packed, "gz", tile, x * ny + y)
        return packed

    packed = lax.fori_loop(0, nx, body, [jnp.zeros((ns, nz), f32) for _ in refs])
    for ref, value in zip(refs, packed):
        ref[...] = value


def copy_faces(faces, field, shape, extra):
    _, nx, ny, nz = shape
    slab = ny * nz
    for refs, axis, width, count, last in (
        (faces[0], "gx", slab, 1, (nx - 1) * slab),
        (faces[1], "gy", nz, nx, slab - nz),
    ):
        for i, ref in enumerate(refs):
            at = pl.multiple_of(jnp.where(faces_up(axis, i), last, 0), nz)
            for j in range(count):
                ref[:, j * width : (j + 1) * width] = field[:, pl.ds(at + j * slab, width)]
        if refs and axis in extra:
            refs[0][:, count * width :] = extra[axis]


def pack_symmetric(square, rows):
    n = square.shape[0]
    half = n // 2
    low = square[half:, half:]
    low = jnp.concatenate([low[: half // 2], low[half // 2 :]], axis=1)
    whole = jnp.concatenate([square[:half], low], axis=0)
    return jnp.concatenate([whole[i : i + rows] for i in range(0, whole.shape[0], rows)], axis=1)


def unpack_symmetric(rows):
    n = rows.shape[1]
    half = n // 2
    low = rows[half:]
    low = jnp.concatenate([low[:, :half], low[:, half:]], axis=0)
    corner = rows[:half, half:]
    return jnp.concatenate([rows[:half], jnp.concatenate([corner.T, low], axis=1)], axis=0)


def pack_square(square, lanes):
    rows = square.shape[0] ** 2 // lanes
    return jnp.concatenate([square[i : i + rows] for i in range(0, square.shape[0], rows)], axis=1)


def unpack_square(rows, n):
    return jnp.concatenate([rows[:, i : i + n] for i in range(0, rows.shape[1], n)], axis=0)


def face_shapes(shape, extra=(), width=0):
    ns, nx, ny, nz = shape
    out = []
    for axis, lanes in (("gx", ny * nz), ("gy", nx * nz), ("gz", nz)):
        n = face_count(axis)
        out.append([(ns, lanes + (width if i == 0 and axis in extra else 0)) for i in range(n)])
    return out


def unflatten(flat):
    out = []
    for axis in ("gx", "gy", "gz"):
        n = face_count(axis)
        out.append(list(flat[:n]))
        flat = flat[n:]
    return out, flat


def exchange(faces):
    got = {}
    for axis, sent in reversed(list(zip(("gx", "gy", "gz"), faces, strict=True))):
        size = lax.axis_size(axis)
        got[axis] = []
        for i, face in enumerate(sent):
            pairs = [(j, j + 1) for j in range(i, size - 1, 2)]
            pairs = pairs + [(j, i) for i, j in pairs]
            got[axis].append(lax.ppermute(face, axis, pairs))
    return [got["gx"], got["gy"], got["gz"]]


def start_kernel(shape, nk, reduced, basis, fine, bound, on, off, inlet, out_a, out_bb, out_bound, out_rates, *rest):
    ns, nx, ny, nz = shape
    both, rest = rest[:nx], rest[nx:]
    faces, scratch = unflatten(rest)
    r_buf, b_buf, f_buf, rows, on_buf, off_buf, inlet_buf, r_sem, b_sem, f_sem, bound_sem, rate_sem = scratch
    rate_bufs = (on_buf, off_buf, inlet_buf)
    rate_copies = [
        pltpu.make_async_copy(a, b, rate_sem.at[i])
        for i, (a, b) in enumerate(zip((on, off, inlet), rate_bufs))
    ]
    bound_copy = lambda x: pltpu.make_async_copy(bound.at[:, x], out_bound.at[x], bound_sem.at[x])
    r_copy = pltpu.make_async_copy(reduced, r_buf, r_sem)
    f_copy = pltpu.make_async_copy(fine, f_buf, f_sem)
    b_copy = lambda x: pltpu.make_async_copy(basis.at[:, x], b_buf.at[x], b_sem.at[x])
    r_copy.start()
    b_copy(0).start()
    f_copy.start()
    for x in range(1, nx):
        b_copy(x).start()
    for copy in rate_copies:
        copy.start()
    for x in range(nx):
        bound_copy(x).start()
    r_copy.wait()
    r_high, r_low = split(r_buf[...])
    r_all = stacked(r_high, r_low)
    for copy in rate_copies:
        copy.wait()
    lane = lax.broadcasted_iota(jnp.int32, (ns, ns), 1)
    own = lax.broadcasted_iota(jnp.int32, (ns, ns), 0) == lane
    column = lambda ref: jnp.sum(
        jnp.where(own, jnp.broadcast_to(ref[...], (ns, ns)), 0.0), axis=1, keepdims=True
    )
    lane = lax.broadcasted_iota(jnp.int32, out_rates.shape, 1)
    out_rates[...] = jnp.where(
        lane == 0, column(on_buf), jnp.where(lane == 1, column(off_buf), column(inlet_buf))
    )
    group = max(1, min(ny, 256 // nz))

    def body(x, packed):
        if x % 4 == 0:
            for i in range(x, min(x + 4, nx)):
                b_copy(i).wait()
        if x == 0:
            f_copy.wait()
        flat = b_buf.at[x].reshape(nk * ny, nz)
        rows[...] = f_buf[:, pl.ds(x, 1)].reshape(ns * ny, nz).astype(f32)
        for y in range(0, ny, group):
            at = (x * ny + y) * nz
            parts = [split(flat[pl.ds(y + i, nk, stride=ny), :]) for i in range(group)]
            high = jnp.concatenate([p[0] for p in parts], axis=1)
            low = jnp.concatenate([p[1] for p in parts], axis=1)
            both[x][:nk, pl.ds(y * nz, group * nz)] = high
            both[x][nk:, pl.ds(y * nz, group * nz)] = low
            slab = mm(r_all, jnp.concatenate([high, low], axis=0))
            slab = slab[:ns] + slab[ns:]
            for i in range(group):
                tile = slab[:, i * nz : (i + 1) * nz] + rows[pl.ds(y + i, ns, stride=ny), :]
                out_a[:, pl.ds(at + i * nz, nz)] = tile
                packed = pack_column(packed, "gz", tile, x * ny + y + i)
        return packed

    packed = [jnp.zeros((ns, nz), f32) for _ in faces[2]]
    for x in range(nx):
        packed = body(x, packed)
    for ref, value in zip(faces[2], packed):
        ref[...] = value
    product = sum(mm_nt(piece[:nk, :], piece[...]) for piece in both)
    mixed = product[:, nk:]
    out_bb[...] = pack_symmetric(product[:, :nk] + mixed + mixed.T, ns)
    copy_faces(faces, out_a, shape, {"gy": out_bb[...]} if doubling("gy") else {})
    for x in range(nx):
        bound_copy(x).wait()


def start(reduced, basis, fine, bound, rates):
    nk = basis.shape[0]
    ns, nx, ny, nz = shape = fine.shape
    width = nk * nk * 3 // 4 // ns
    groups = [s for g in face_shapes(shape, ["gy"] if doubling("gy") else [], width) for s in g]
    outs = pl.pallas_call(
        functools.partial(start_kernel, shape, nk),
        in_specs=[pl.BlockSpec(memory_space=pltpu.HBM)] * 7,
        out_specs=[
            pl.BlockSpec(memory_space=pltpu.VMEM) for _ in range(4 + nx + len(groups))
        ],
        out_shape=[
            jax.ShapeDtypeStruct((ns, nx * ny * nz), f32),
            jax.ShapeDtypeStruct((ns, width), f32),
            jax.ShapeDtypeStruct((nx, ns, ny, nz), f32),
            jax.ShapeDtypeStruct((ns, nz), f32),
        ]
        + [jax.ShapeDtypeStruct((2 * nk, ny * nz), bf16)] * nx
        + [jax.ShapeDtypeStruct(s, f32) for s in groups],
        scratch_shapes=[
            pltpu.VMEM((ns, nk), f32),
            pltpu.VMEM((nx, nk, ny, nz), f32),
            pltpu.VMEM((ns, nx, ny, nz), bf16),
            pltpu.VMEM((ns * ny, nz), f32),
            pltpu.VMEM((1, ns), f32),
            pltpu.VMEM((1, ns), f32),
            pltpu.VMEM((1, ns), f32),
            pltpu.SemaphoreType.DMA,
            pltpu.SemaphoreType.DMA((nx,)),
            pltpu.SemaphoreType.DMA,
            pltpu.SemaphoreType.DMA((nx,)),
            pltpu.SemaphoreType.DMA((3,)),
        ],
        compiler_params=pltpu.CompilerParams(vmem_limit_bytes=vmem_limit),
        name="start",
    )(*[pltpu.with_memory_space_constraint(a, pltpu.HBM) for a in (reduced, basis, fine, bound, *rates)])
    faces, _ = unflatten(outs[4 + nx :])
    return outs[:4], outs[4 : 4 + nx], faces


def beside_of(got, axis, before):
    if len(got) == 1:
        return got[0][...]
    return jnp.where(faces_up(axis, 1 if before else 0), got[1][...], got[0][...])


def stencil(shape, x, pad, y_got, z_got, bound_tile, store, args):
    velocity, zone_labels, capacity, rates = args
    ns, nx, ny, nz = shape
    first = {a: lax.axis_index(a) == 0 for a in ("gy", "gz")}
    last = {a: lax.axis_index(a) == lax.axis_size(a) - 1 for a in ("gy", "gz")}
    labels = zone_labels[x]
    cap_slab = jnp.zeros(labels.shape, f32)
    for zone in range(capacity.shape[0]):
        cap_slab = cap_slab + jnp.where(labels == zone + 1, capacity[zone], 0.0)
    surface_slab = jnp.where(cap_slab > 0.0, 1.0, 0.0)
    velocity_slab = velocity[x]
    on = jnp.broadcast_to(rates[:, 0:1], (ns, nz))
    off = jnp.broadcast_to(rates[:, 1:2], (ns, nz))
    lane = lax.broadcasted_iota(jnp.int32, (ns, nz), 1)
    x_at = aligned(x * nz, nz)
    y_at = [ref.at[:, pl.ds(x_at, nz)] for ref in y_got]
    left, right = lane == 0, lane == nz - 1
    inner = lane == jnp.where(first["gz"], nz - 1, 0)
    inner_low = lane == jnp.where(first["gz"], -1, 0)
    inner_high = lane == jnp.where(last["gz"], -1, nz - 1)
    for y in range(ny):
        at = aligned(x * ny * nz, nz) + y * nz
        tile = lambda slabs_on, rows_on: pad[
            :, pl.ds(aligned(at + (slabs_on * ny + rows_on) * nz, nz), nz)
        ]
        centre, behind, ahead = tile(1, 0), tile(0, 0), tile(2, 0)
        if y > 0:
            y_low = tile(1, -1)
        elif y_got:
            y_low = jnp.where(first["gy"], centre, beside_of(y_at, "gy", True))
        else:
            y_low = centre
        if y < ny - 1:
            y_high = tile(1, 1)
        elif y_got:
            y_high = jnp.where(last["gy"], centre, beside_of(y_at, "gy", False))
        else:
            y_high = centre
        z_low, z_high = pltpu.roll(centre, 1, 1), pltpu.roll(centre, nz - 1, 1)
        cell = x * ny + y
        edge = centre
        if len(z_got) == 1:
            shift = jnp.where(first["gz"], nz - 1 - cell, lax.rem(nz - cell, nz))
            edge = jnp.where(inner, pltpu.roll(z_got[0][...], shift, 1), edge)
        elif len(z_got) == 2:
            beside = pltpu.roll(beside_of(z_got, "gz", True), lax.rem(nz - cell, nz), 1)
            edge = jnp.where(inner_low, beside, edge)
            beside = pltpu.roll(beside_of(z_got, "gz", False), nz - 1 - cell, 1)
            edge = jnp.where(inner_high, beside, edge)
        z_low = jnp.where(left, edge, z_low)
        z_high = jnp.where(right, edge, z_high)
        near = behind + ahead + y_low + y_high + z_low + z_high
        row = lambda slab: jnp.broadcast_to(slab[y : y + 1], (ns, nz))
        bound_now = bound_tile(y, at)
        reaction = row(surface_slab) * (
            on * centre * (row(cap_slab) - bound_now) - off * bound_now
        )
        moved = (
            centre
            + diffusion_number * (near - 6.0 * centre)
            - row(velocity_slab) * (centre - behind)
            - reaction
        )
        store(cell, y, at, moved, bound_now + reaction)


def fill_pad(shape, pad, analyte, x_got, rates):
    ns, nx, ny, nz = shape
    slab = ny * nz
    pad[:, slab : (nx + 1) * slab] = analyte[...]
    end = (nx + 1) * slab
    for i, ref in enumerate(x_got):
        at = pl.multiple_of(jnp.where(faces_up("gx", i), end, 0), slab)
        pad[:, pl.ds(at, slab)] = ref[:, :slab]

    @pl.when(lax.axis_index("gx") == 0)
    def _():
        pad[:, :slab] = jnp.broadcast_to(rates[:, 2:3], (ns, slab))

    @pl.when(lax.axis_index("gx") == lax.axis_size("gx") - 1)
    def _():
        pad[:, end:] = analyte[:, (nx - 1) * slab :]


def first_kernel(shape, analyte, bound, velocity, zone_labels, capacity, rates, bb, *rest):
    ns, nx, ny, nz = shape
    got, rest = unflatten(rest)
    out_a, out_bound, out_bb = rest[:3]
    faces, (pad,) = unflatten(rest[3:])
    fill_pad(shape, pad, analyte, got[0], rates)

    def body(x):

        rows = bound.at[x].reshape(ns * ny, nz)

        def bound_tile(y, at):
            return rows[pl.ds(y, ns, stride=ny), :]

        def store(cell, y, at, moved, bound_then):
            out_bound[:, pl.ds(at, nz)] = bound_then
            out_a[:, pl.ds(at, nz)] = moved

        stencil(
            shape, x, pad, got[1], got[2], bound_tile, store, (velocity, zone_labels, capacity, rates)
        )
    for x in range(nx):
        body(x)
    pack_columns(faces[2], out_a, shape)
    out_bb[...] = bb[...] + got[1][0][:, nx * nz :] if doubling("gy") else bb[...]
    copy_faces(faces, out_a, shape, {"gx": out_bb[...]} if doubling("gx") else {})


def second_kernel(shape, nk, analyte, bound, velocity, zone_labels, capacity, rates, bb, *rest):
    ns, nx, ny, nz = shape
    both, rest = rest[:nx], rest[nx:]
    got, rest = unflatten(rest)
    out_s, out_bound, out_totals, out_bb, pad, bound_buf, sem = rest
    fill_pad(shape, pad, analyte, got[0], rates)

    def body(x, carry):
        rows = bound_buf.at[x].reshape(ns * ny, nz)

        def bound_tile(y, at):
            return bound[:, pl.ds(at, nz)]

        def store(cell, y, at, moved, bound_then):
            rows[pl.ds(y, ns, stride=ny), :] = bound_then
            high, low = split(moved)
            out_s[:ns, pl.ds(at, nz)] = high
            out_s[ns:, pl.ds(at, nz)] = low

        stencil(
            shape, x, pad, got[1], got[2], bound_tile, store, (velocity, zone_labels, capacity, rates)
        )
        copy(x).start()
        return carry

    copy = lambda x: pltpu.make_async_copy(bound_buf.at[x], out_bound.at[:, x], sem.at[x])
    for x in range(nx):
        body(x, 0)
    snap = out_s[...]
    slab = ny * nz
    product = sum(mm_nt(out_s[:, x * slab : (x + 1) * slab], both[x][...]) for x in range(nx))
    out_totals[:ns, :] = product[:ns, :nk] + product[:ns, nk:] + product[ns:, :nk]
    square = mm_nt(snap, snap)
    square = square[:ns, :ns] + square[:ns, ns:] + square[ns:, :ns]
    out_totals[ns:, :] = pack_square(square, nk)
    total = bb[...] + got[0][0][:, ny * nz :] if doubling("gx") else bb[...]
    for i in range(total.shape[1] // nk):
        out_bb[i * ns : (i + 1) * ns, :] = total[:, i * nk : (i + 1) * nk]
    for x in range(nx):
        copy(x).wait()


def step_call(kernel, shape, operands, got, out_shape, name, hbm=(), scratch=(), aliases=None):
    ns, nx, ny, nz = shape
    space = {4: pltpu.SMEM}
    flat = [g for group in got for g in group]
    in_specs = [
        pl.BlockSpec(memory_space=space.get(i, pltpu.VMEM))
        for i in range(len(operands) + len(flat))
    ]
    return pl.pallas_call(
        kernel,
        in_specs=in_specs,
        out_specs=[
            pl.BlockSpec(memory_space=pltpu.HBM if i in hbm else pltpu.VMEM)
            for i in range(len(out_shape))
        ],
        out_shape=out_shape,
        scratch_shapes=[pltpu.VMEM((ns, (nx + 2) * ny * nz), f32), *scratch],
        input_output_aliases=aliases or {},
        compiler_params=pltpu.CompilerParams(vmem_limit_bytes=vmem_limit),
        name=name,
    )(*operands, *flat)


def eliminate(gram, width, between):
    n = gram.shape[0]
    sub = lax.broadcasted_iota(jnp.int32, (n, 2 * n), 0)
    lane = lax.broadcasted_iota(jnp.int32, (n, 2 * n), 1)
    unit = jnp.where(sub[:, :n] == lane[:, :n], 1.0, 0.0)
    work = jnp.concatenate([gram, unit], axis=1)
    for start_at in range(0, n, width):
        columns = [
            jnp.broadcast_to(work[:, start_at + i : start_at + i + 1], (n, 2 * n))
            for i in range(width)
        ]
        for i in range(width):
            j = start_at + i
            scale = jnp.where(sub > j, columns[i] / columns[i][j : j + 1, :], 0.0)
            for k in range(i + 1, width):
                columns[k] = columns[k] - scale * columns[k][j : j + 1, :]
            work = work - scale * work[j : j + 1, :]
            between(j)
    pivots = jnp.sum(jnp.where(lane == sub, work, 0.0), axis=1, keepdims=True)
    work = work / jnp.sqrt(pivots)
    return jnp.where(lane[:, :n] >= sub[:, :n], work[:, :n], 0.0), work[:, n:]


def finish_kernel(shape, nk, inverse_rows, totals, snap, *refs):
    ns, nx, ny, nz = shape
    both, (out_modes, out_factor, out_coeffs, *scratch) = refs[:nx], refs[nx:]
    slab = ny * nz
    rest, modes, sem = scratch
    coeffs = totals[:ns, :] * inverse_rows
    out_coeffs[...] = coeffs
    c_high, c_low = split(coeffs)
    c_all = stacked(c_high, c_low)
    squares = ns + ns * ns // nk
    weighted = mm_exact(coeffs, unpack_symmetric(totals[squares:, :] * inverse_rows))
    exact_nt = functools.partial(
        lax.dot_general,
        dimension_numbers=(((1,), (1,)), ((), ())),
        precision=highest,
        preferred_element_type=f32,
    )
    mixed = exact_nt(coeffs, coeffs)
    gram = unpack_square(totals[ns:squares, :] * inverse_rows, ns) - mixed - mixed + exact_nt(weighted, coeffs)

    pieces = 2 * nx if ny % 2 == 0 and 2 * nx <= ns else nx
    width = nx * slab // pieces

    def residual(j):
        if j >= pieces:
            return
        at = slice(j * width, (j + 1) * width)
        value = snap[:ns, at].astype(f32) + snap[ns:, at].astype(f32)
        piece = both[at.start // slab]
        on = slice(at.start % slab, at.start % slab + width)
        product = mm(c_all, piece[:, on])
        value = value - (product[:ns] + product[ns:])
        high, low = split(value)
        rest[:ns, at] = high
        rest[ns:, at] = low

    factor, inverse = eliminate(gram, 8 if ns % 8 == 0 else 1, residual)
    out_factor[...] = factor
    i_high, i_low = split(inverse)
    i_all = stacked(i_high, i_low)
    copy = lambda x: pltpu.make_async_copy(modes.at[x], out_modes.at[:, x], sem.at[x])
    for x in range(nx):
        at = slice(x * slab, (x + 1) * slab)
        value = mm(i_all, rest[:, at])
        value = value[:ns] + value[ns:]
        flat = modes.at[x].reshape(ns * ny, nz)
        for y in range(ny):
            flat[pl.ds(y, ns, stride=ny), :] = value[:, y * nz : (y + 1) * nz]
        copy(x).start()
    for x in range(nx):
        copy(x).wait()


def finish(shape, inverse_rows, totals, snap, both):
    ns, nx, ny, nz = shape
    nk = both[0].shape[0] // 2
    vmem = pl.BlockSpec(memory_space=pltpu.VMEM)
    return pl.pallas_call(
        functools.partial(finish_kernel, shape, nk, inverse_rows),
        in_specs=[vmem] * (2 + nx),
        out_specs=[pl.BlockSpec(memory_space=pltpu.HBM), vmem, vmem],
        out_shape=[
            jax.ShapeDtypeStruct(shape, f32),
            jax.ShapeDtypeStruct((ns, ns), f32),
            jax.ShapeDtypeStruct((ns, nk), f32),
        ],
        scratch_shapes=[
            pltpu.VMEM((2 * ns, nx * ny * nz), bf16),
            pltpu.VMEM((nx, ns, ny, nz), f32),
            pltpu.SemaphoreType.DMA((nx,)),
        ],
        compiler_params=pltpu.CompilerParams(vmem_limit_bytes=vmem_limit),
        name="finish",
    )(totals, snap, *both)


def sum_over(small, large):
    def swapped(value, axis, stride):
        size = lax.axis_size(axis)
        return value + lax.ppermute(value, axis, [(i, i ^ stride) for i in range(size)])

    for axis in ("gy", "gx"):
        if doubling(axis):
            small = swapped(small, axis, 1)
    value = jnp.concatenate([small, large], axis=0)
    for axis in ("gz", "gy", "gx"):
        size = lax.axis_size(axis)
        if not doubling(axis):
            value = lax.psum(value, axis) if size > 1 else value
            continue
        stride = 1 if axis == "gz" else 2
        while stride < size:
            value = swapped(value, axis, stride)
            stride *= 2
    return value


def on_device(
    basis_modes,
    reduced_state,
    fine_state,
    bound_state,
    velocity,
    zone_labels,
    capacity,
    on_rate,
    off_rate,
    inlet_level,
):
    ns, nx, ny, nz = shape = fine_state.shape
    nk = basis_modes.shape[0]
    cells = nx * ny * nz
    rates = [value[None] for value in (on_rate, off_rate, inlet_level)]
    (analyte, bb, bound, rates), both, faces = start(
        reduced_state.T, basis_modes, fine_state, bound_state, rates
    )
    got = exchange(faces)
    fields = [velocity, zone_labels, capacity, rates]
    struct = jax.ShapeDtypeStruct
    outs = step_call(
        functools.partial(first_kernel, shape),
        shape,
        [analyte, bound] + fields + [bb],
        got,
        [struct((ns, cells), f32), struct((ns, cells), f32), struct(bb.shape, f32)]
        + [
            struct(s, f32)
            for g in face_shapes(shape, ["gx"] if doubling("gx") else [], bb.shape[1])
            for s in g
        ],
        "first_step",
    )
    faces, _ = unflatten(outs[3:])
    got = exchange(faces)
    snap, bound_next, small, large = step_call(
        functools.partial(second_kernel, shape, nk),
        shape,
        [outs[0], outs[1]] + fields + [outs[2], *both],
        got,
        [
            struct((2 * ns, cells), bf16),
            struct(shape, f32),
            struct((ns + ns * ns // nk, nk), f32),
            struct((bb.size // nk, nk), f32),
        ],
        "second_step",
        hbm=(1,),
        scratch=[
            pltpu.VMEM((nx, ns, ny, nz), f32),
            pltpu.SemaphoreType.DMA((nx,)),
        ],
    )
    totals = sum_over(small, large)
    inverse_rows = 1.0 / (
        cells * lax.axis_size("gx") * lax.axis_size("gy") * lax.axis_size("gz")
    )
    modes, factor, coeffs = finish(shape, inverse_rows, totals, snap, both)
    return (modes, factor, coeffs.T, bound_next)


def solution(mesh):
    return jax.shard_map(
        on_device,
        mesh=mesh,
        in_specs=(
            P(None, ("grp", "gx"), "gy", "gz"),
            P("grp", None),
            P(None, ("grp", "gx"), "gy", "gz"),
            P(None, ("grp", "gx"), "gy", "gz"),
            P(("grp", "gx"), "gy", "gz"),
            P(("grp", "gx"), "gy", "gz"),
            P(),
            P(),
            P(),
            P("grp"),
        ),
        out_specs=(
            P(None, ("grp", "gx"), "gy", "gz"),
            P("grp", None),
            P("grp", None),
            P(None, ("grp", "gx"), "gy", "gz"),
        ),
        check_vma=False,
    )
```
